512 devices in a mesh: left: 16 (over x, y_hi, core), right: 32 (over y_lo, z).
Axes of the slice: x: 4, y: 8 (y_hi: 2, y_lo: 4; y = y_hi * 4 + y_lo), z: 8, core: 2. Of those that a mesh axis runs over, the one named last changes fastest.
Arguments:
- left_table: bfloat16 [32768, 256], P('left'), may hold values from -1.5 to 1.5
- right_table: bfloat16 [16, 16384, 256], P('left', 'right'), may hold values from -1.5 to 1.5
- relations: float32 [512, 256], replicated, may hold values from -6 to 6
- source_ids: int32 [16, 32, 1024], P('left', 'right'), may hold values from 0 to 2047
- relation_ids: int32 [16, 32, 1024], P('left', 'right'), may hold values from 0 to 511
- target_ids: int32 [16, 32, 1024], P('left', 'right'), may hold values from 0 to 511
- negative_ids: int32 [16, 32, 1, 1024], P('left', 'right'), may hold values from 0 to 511
- edge_counts: int32 [16, 32], P('left', 'right'), may hold values from 1 to 1024
Outputs:
- left_next: bfloat16 [32768, 256], P('left')
- right_next: bfloat16 [16, 16384, 256], P('left', 'right')
- relations_next: float32 [512, 256], replicated
The draws below stay inside these ranges and needn't reach their ends.
Inputs may be any that keep to these rules, and one draw needn't show every extreme that they name: Edge slots at positions from edge_counts to 1023 hold ids but are padding.
All inputs are finite; a program needn't handle non-finite values.
Results may differ from the reference program's by a relative error of at most 0.0013.
Values may be sent and summed in bfloat16 or wider, within the bound.
No kernel may reach another device: no remote copies, remote signals or barrier semaphores. Data moves between devices by JAX's collectives and lax.ppermute only.
A program may use at most 64 MiB of HBM per device.

```python
import math
import jax
import jax.numpy as jnp
import numpy as np
from jax import lax

D = 256
REL = 512
NEG = 1024
GROUP = 1024
GROUPS = 1
ENT_L = 2048
ENT_R = 512
EDGE_CAP = 1024
LEFT_PARTS = 16
RIGHT_PARTS = 32
LEFT_ROWS = 32768
RIGHT_ROWS = 16384
N_LEFT = 16
N_RIGHT = 32


def touch_ends(entries, stream_key, least, top_value):
    place = [jax.random.randint(jax.random.fold_in(stream_key, axis), (), 0, length) for axis, length in enumerate(entries.shape)]
    widest = entries.shape.index(max(entries.shape))
    neighbour = place[:widest] + [(place[widest] + 1) % entries.shape[widest]] + place[widest + 1:]
    return entries.at[tuple(place)].set(least).at[tuple(neighbour)].set(top_value)


def block_levels(rng, extent, shards, smallest, largest):
    def one(dim, parts):
        draws = jax.random.uniform(jax.random.fold_in(jax.random.fold_in(rng, 6), dim), (parts,), jnp.float32, smallest / len(shards), largest / len(shards))
        return jnp.repeat(jnp.exp(draws), extent[dim] // parts).reshape((-1,) + (1,) * (len(extent) - dim - 1))

    gain = one(*shards[0])
    for cut in shards[1:]:
        gain = gain * one(*cut)
    return gain


def rank_table(amount, slope):
    weights = [(1 << 20) // math.isqrt(rank ** slope) + 1 for rank in range(1, amount + 1)]
    spread = 1 + sum(weights) // (1 << 30)
    return np.cumsum(np.array([max(1, weight // spread) for weight in weights]))


def ranked_ids(own_key, dims, amount, slope):
    grid = rank_table(amount, slope)
    pick = jax.random.randint(jax.random.fold_in(own_key, 1), dims, 0, int(grid[amount - 1]))
    grade = jnp.searchsorted(jnp.asarray(grid, jnp.int32), pick, side="right")
    return jax.random.permutation(jax.random.fold_in(own_key, 2), amount)[grade].astype(jnp.int32)


def gaussian(stream_key, dims, deviation, bound, pieces=(), kind=jnp.bfloat16):
    result = deviation * jax.random.normal(stream_key, dims, jnp.float32)
    if pieces:
        result = result * block_levels(stream_key, dims, pieces, -0.22, 0.18)
    return jnp.clip(result, -bound, bound).astype(kind)


def setup_inputs(seed: int = 0) -> dict:
    splits = jax.random.split(jax.random.key(seed), 9)
    return {
        "left_table": gaussian(splits[0], (LEFT_ROWS, D), 0.25, 1.5, ((0, 16),)),
        "right_table": gaussian(splits[1], (LEFT_PARTS, RIGHT_ROWS, D), 0.25, 1.5, ((0, 16), (1, 32))),
        "relations": gaussian(splits[2], (REL, D), 1.0, 6.0, (), jnp.float32),
        "source_ids": touch_ends(jax.random.randint(splits[3], (LEFT_PARTS, RIGHT_PARTS, EDGE_CAP), 0, ENT_L), jax.random.fold_in(splits[3], 1), 0, ENT_L - 1).astype(jnp.int32),
        "relation_ids": touch_ends(ranked_ids(splits[4], (LEFT_PARTS, RIGHT_PARTS, EDGE_CAP), REL, 2), jax.random.fold_in(splits[4], 3), 0, REL - 1).astype(jnp.int32),
        "target_ids": touch_ends(jax.random.randint(splits[5], (LEFT_PARTS, RIGHT_PARTS, EDGE_CAP), 0, ENT_R), jax.random.fold_in(splits[5], 1), 0, ENT_R - 1).astype(jnp.int32),
        "negative_ids": touch_ends(jax.random.randint(splits[6], (LEFT_PARTS, RIGHT_PARTS, GROUPS, NEG), 0, ENT_R), jax.random.fold_in(splits[6], 1), 0, ENT_R - 1).astype(jnp.int32),
        "edge_counts": touch_ends(jax.random.randint(splits[7], (LEFT_PARTS, RIGHT_PARTS), 1, EDGE_CAP + 1), jax.random.fold_in(splits[7], 1), 1, EDGE_CAP).astype(jnp.int32),
    }


step_size = 0.5
relation_step = 12.0


def block_terms(left_blk, right_blk, relations, src, kind, dst, neg, live):
    half = relations.shape[1] // 2
    head = left_blk[src].astype(jnp.float32)
    tail = right_blk[dst].astype(jnp.float32)
    rel = relations[kind]
    hre, him = head[:, :half], head[:, half:]
    rre, rim = rel[:, :half], rel[:, half:]
    query = jnp.concatenate([hre * rre - him * rim, hre * rim + him * rre], axis=1)
    q_low = query.astype(jnp.bfloat16)
    pos = jnp.sum(query * tail, axis=1)
    negrows = right_blk[neg]
    scores = jnp.dot(q_low, negrows.T, preferred_element_type=jnp.float32)
    c_pos = -jax.nn.sigmoid(-pos) * live
    c_neg = (jax.nn.sigmoid(scores) * (live[:, None] / neg.shape[0])).astype(jnp.bfloat16)
    g_query = jnp.dot(c_neg, negrows, preferred_element_type=jnp.float32) + c_pos[:, None] * tail
    g_neg = jnp.dot(c_neg.T, q_low, preferred_element_type=jnp.float32)
    g_tail = c_pos[:, None] * query
    gre, gim = g_query[:, :half], g_query[:, half:]
    grad_h = jnp.concatenate([gre * rre + gim * rim, -gre * rim + gim * rre], axis=1)
    grad_r = jnp.concatenate([gre * hre + gim * him, -gre * him + gim * hre], axis=1)
    return grad_h, grad_r, g_tail, g_neg


def bucket(left_blk, right_blk, relations, src, kind, dst, negs, count):
    def one(carry, index):
        lgrad, rgrad, tgrad = carry
        start = index * GROUP
        s = lax.dynamic_slice_in_dim(src, start, GROUP)
        k = lax.dynamic_slice_in_dim(kind, start, GROUP)
        d = lax.dynamic_slice_in_dim(dst, start, GROUP)
        n = negs[index]
        live = ((start + jnp.arange(GROUP, dtype=jnp.int32)) < count).astype(jnp.float32)
        grad_h, grad_r, g_tail, g_neg = block_terms(left_blk, right_blk, relations, s, k, d, n, live)
        lgrad = lgrad.at[s].add(grad_h)
        rgrad = rgrad.at[k].add(grad_r)
        tgrad = tgrad.at[d].add(g_tail).at[n].add(g_neg)
        return (lgrad, rgrad, tgrad), None
    init = (jnp.zeros(left_blk.shape, jnp.float32), jnp.zeros(relations.shape, jnp.float32), jnp.zeros(right_blk.shape, jnp.float32))
    out, unused = lax.scan(one, init, jnp.arange(GROUPS, dtype=jnp.int32))
    return out


def reference(left_table, right_table, relations, source_ids, relation_ids, target_ids, negative_ids, edge_counts):
    lefts = left_table.reshape(N_LEFT, ENT_L, D)
    rights = right_table.reshape(N_LEFT, N_RIGHT, ENT_R, D)

    def per_left(items):
        left_blk, right_row, src_row, kind_row, dst_row, neg_row, count_row = items

        def per_bucket(carry, xs):
            lsum, rsum = carry
            right_blk, src, kind, dst, negs, count = xs
            lgrad, rgrad, tgrad = bucket(left_blk, right_blk, relations, src, kind, dst, negs, count)
            updated = (right_blk.astype(jnp.float32) - step_size * tgrad).astype(jnp.bfloat16)
            return (lsum + lgrad, rsum + rgrad), updated
        init = (jnp.zeros((ENT_L, D), jnp.float32), jnp.zeros((REL, D), jnp.float32))
        (lsum, rsum), updated = lax.scan(per_bucket, init, (right_row, src_row, kind_row, dst_row, neg_row, count_row))
        new_left = (left_blk.astype(jnp.float32) - step_size * lsum).astype(jnp.bfloat16)
        return new_left, rsum, updated

    new_lefts, rel_parts, updated = lax.map(per_left, (lefts, rights, source_ids, relation_ids, target_ids, negative_ids, edge_counts))
    rel_total = jnp.sum(rel_parts, axis=0)
    right_next = jnp.roll(updated, 1, axis=1).reshape(N_LEFT, N_RIGHT * ENT_R, D)
    relations_next = relations - relation_step * rel_total
    return new_lefts.reshape(N_LEFT * ENT_L, D), right_next, relations_next
```

```python
import functools

import jax
import jax.numpy as jnp
from jax import lax
from jax.experimental import pallas as pl
from jax.experimental.pallas import tpu as pltpu
from jax.sharding import PartitionSpec as P

step_size = 0.5
relation_step = 12.0
EDGES = 256
ROWS = 256
F32 = jnp.float32
BF16 = jnp.bfloat16


def passed_along(array, axis, by):
    peers = lax.axis_size(axis)
    return lax.ppermute(array, axis, [(i, (i + by) % peers) for i in range(peers)])


def mm(a, b):
    return lax.dot_general(a, b, (((1,), (0,)), ((), ())), preferred_element_type=F32)


def mm_nt(a, b):
    return lax.dot_general(a, b, (((1,), (1,)), ((), ())), preferred_element_type=F32)


def two_parts(x):
    high = x.astype(BF16)
    return high, (x - high.astype(F32)).astype(BF16)


def one_hot(rows, ids):
    return jnp.where(lax.broadcasted_iota(jnp.int32, (rows, ids.shape[1]), 0) == ids, 1.0, 0.0)


def bucket_kernel(
    count_ref, src_ref, kind_ref, dst_ref, neg_ref, left_ref, right_ref, rel_ref,
    lgrad_ref, rgrad_ref, right_new_ref,
    oh_src, gh_high, gh_low, left_t, right_t, rel_high_t, rel_low_t, tgrad,
):
    n_left, width = left_ref.shape
    n_right, n_rel = right_ref.shape[0], rel_ref.shape[0]
    half = width // 2
    blocks = src_ref.shape[0]
    negs = neg_ref.shape[0] * neg_ref.shape[2]
    count = count_ref[0]
    eye = jnp.where(
        lax.broadcasted_iota(jnp.int32, (width, width), 0)
        == lax.broadcasted_iota(jnp.int32, (width, width), 1),
        1.0,
        0.0,
    ).astype(BF16)
    left_t[...] = mm_nt(eye, left_ref[...]).astype(BF16)
    right_t[...] = mm_nt(eye, right_ref[...]).astype(BF16)
    rel_high, rel_low = two_parts(rel_ref[...])
    rel_high_t[...] = mm_nt(eye, rel_high).astype(BF16)
    rel_low_t[...] = mm_nt(eye, rel_low).astype(BF16)
    seen = one_hot(n_right, neg_ref[0])
    for i in range(1, neg_ref.shape[0]):
        seen = seen + one_hot(n_right, neg_ref[i])
    times = jnp.sum(seen, axis=1, keepdims=True) * (1.0 / negs)
    rgrad_ref[...] = jnp.zeros_like(rgrad_ref)
    tgrad[...] = jnp.zeros_like(tgrad)

    def block(i, carry):
        ohs = one_hot(n_left, src_ref[i]).astype(BF16)
        ohk = one_hot(n_rel, kind_ref[i]).astype(BF16)
        ohd = one_hot(n_right, dst_ref[i]).astype(BF16)
        oh_src[i] = ohs
        head = mm(left_t[...], ohs)
        tail = mm(right_t[...], ohd)
        rel = mm(rel_high_t[...], ohk) + mm(rel_low_t[...], ohk)
        hre, him = head[:half], head[half:]
        rre, rim = rel[:half], rel[half:]
        query = jnp.concatenate([hre * rre - him * rim, hre * rim + him * rre], axis=0)
        q_low = query.astype(BF16)
        pos = jnp.sum(query * tail, axis=0, keepdims=True)
        slot = i * EDGES + lax.broadcasted_iota(jnp.int32, (1, EDGES), 1)
        live = jnp.where(slot < count, 1.0, 0.0)
        c_pos = -jax.nn.sigmoid(-pos) * live
        scores = mm(right_ref[...], q_low)
        c_neg = (jax.nn.sigmoid(scores) * (times * live)).astype(BF16)
        g_query = mm(right_t[...], c_neg) + c_pos * tail
        gre, gim = g_query[:half], g_query[half:]
        grad_h = jnp.concatenate([gre * rre + gim * rim, -gre * rim + gim * rre], axis=0)
        grad_r = jnp.concatenate([gre * hre + gim * him, -gre * him + gim * hre], axis=0)
        gh_high[i], gh_low[i] = two_parts(grad_h)
        rgrad_ref[...] += mm_nt(ohk, grad_r.astype(BF16))
        t_high, t_low = two_parts(c_pos * query)
        tgrad[...] += mm_nt(c_neg, q_low) + mm_nt(ohd, t_high) + mm_nt(ohd, t_low)
        return carry

    lax.fori_loop(0, blocks, block, 0)
    right_new_ref[...] = (right_ref[...].astype(F32) - step_size * tgrad[...]).astype(BF16)

    def rows(j, carry):
        at = pl.ds(pl.multiple_of(j * ROWS, ROWS), ROWS)
        total = jnp.zeros((ROWS, width), F32)
        for i in range(blocks):
            hot = oh_src[i, at, :]
            total += mm_nt(hot, gh_high[i]) + mm_nt(hot, gh_low[i])
        lgrad_ref[at, :] = total
        return carry

    lax.fori_loop(0, n_left // ROWS, rows, 0)


def bucket_grads(count, src, kind, dst, neg, left_blk, right_blk, relations, interpret=False):
    n_left, width = left_blk.shape
    n_right, n_rel, edges = right_blk.shape[0], relations.shape[0], src.size
    blocks = edges // EDGES
    vmem = pl.BlockSpec(memory_space=pltpu.VMEM)
    return pl.pallas_call(
        bucket_kernel,
        out_shape=(
            jax.ShapeDtypeStruct((n_left, width), F32),
            jax.ShapeDtypeStruct((n_rel, width), F32),
            jax.ShapeDtypeStruct((n_right, width), BF16),
        ),
        in_specs=[pl.BlockSpec(memory_space=pltpu.SMEM)] + [vmem] * 7,
        out_specs=(vmem, vmem, vmem),
        scratch_shapes=[
            pltpu.VMEM((blocks, n_left, EDGES), BF16),
            pltpu.VMEM((blocks, width, EDGES), BF16),
            pltpu.VMEM((blocks, width, EDGES), BF16),
            pltpu.VMEM((width, n_left), BF16),
            pltpu.VMEM((width, n_right), BF16),
            pltpu.VMEM((width, n_rel), BF16),
            pltpu.VMEM((width, n_rel), BF16),
            pltpu.VMEM((n_right, width), F32),
        ],
        interpret=interpret,
        name="bucket",
    )(
        count,
        src.reshape(blocks, 1, EDGES),
        kind.reshape(blocks, 1, EDGES),
        dst.reshape(blocks, 1, EDGES),
        neg.reshape(-1, 1, EDGES),
        left_blk,
        right_blk,
        relations,
    )


def to_all(rows, axis):
    peers = lax.axis_size(axis)
    copies = jnp.broadcast_to(rows[None], (peers,) + rows.shape)
    return lax.all_to_all(copies, axis, 0, 0)


def shards(
    left_table, right_table, relations, source_ids, relation_ids, target_ids, negative_ids, edge_counts
):
    left_grad, rel_grad, updated = bucket_grads(
        edge_counts.reshape(1), source_ids, relation_ids, target_ids, negative_ids,
        left_table, right_table[0], relations,
    )
    width = relations.shape[1]
    moved = passed_along(updated, "right", 1)
    peers = lax.axis_size("right")
    mine = lax.axis_index("right")
    own_left = left_table.shape[0] // peers
    own_rel = relations.shape[0] // peers
    sent = jnp.concatenate(
        [left_grad.reshape(peers, own_left, width), rel_grad.reshape(peers, own_rel, width)], axis=1
    ).astype(jnp.float16)
    got = lax.all_to_all(sent, "right", 0, 0)
    total = jnp.sum(got.astype(F32), axis=0)
    left_rows = lax.dynamic_slice_in_dim(left_table, mine * own_left, own_left, 0)
    left_rows = (left_rows.astype(F32) - step_size * total[:own_left]).astype(BF16)
    rel_total = jnp.sum(to_all(total[own_left:], "left"), axis=0)
    rel_rows = lax.dynamic_slice_in_dim(relations, mine * own_rel, own_rel, 0)
    rel_rows = rel_rows - relation_step * rel_total
    high = lax.reduce_precision(rel_rows, 8, 7)
    low = (rel_rows - high).astype(BF16)
    out = to_all(jnp.concatenate([left_rows, high.astype(BF16), low], axis=0), "right")
    left_next = out[:, :own_left].reshape(left_table.shape)
    high, low = out[:, own_left : own_left + own_rel], out[:, own_left + own_rel :]
    relations_next = (high.astype(F32) + low.astype(F32)).reshape(relations.shape)
    return (left_next, moved[None], relations_next)


def solution(mesh):
    return jax.shard_map(
        shards,
        mesh=mesh,
        in_specs=(
            P("left", None),
            P("left", "right", None),
            P(),
            P("left", "right", None),
            P("left", "right", None),
            P("left", "right", None),
            P("left", "right", None, None),
            P("left", "right"),
        ),
        out_specs=(P("left", None), P("left", "right", None), P()),
        check_vma=False,
    )
```

```python
import jax
import jax.numpy as jnp
from jax import lax
from jax.experimental import pallas as pl
from jax.experimental.pallas import tpu as pltpu
from jax.sharding import PartitionSpec as P


step_size = 0.5
relation_step = 12.0
EDGES = 256
ROWS = 256
F32 = jnp.float32
BF16 = jnp.bfloat16


def passed_along(array, axis, by):
    peers = lax.axis_size(axis)
    return lax.ppermute(array, axis, [(i, (i + by) % peers) for i in range(peers)])


def mm(a, b):
    return lax.dot_general(a, b, (((1,), (0,)), ((), ())), preferred_element_type=F32)


def mm_nt(a, b):
    return lax.dot_general(a, b, (((1,), (1,)), ((), ())), preferred_element_type=F32)


def two_parts(x):
    high = x.astype(BF16)
    return high, (x - high.astype(F32)).astype(BF16)


def one_hot(rows, ids):
    return jnp.where(lax.broadcasted_iota(jnp.int32, (rows, ids.shape[1]), 0) == ids, 1.0, 0.0)


def edge_kernel(
    count_ref, src_ref, kind_ref, dst_ref, neg_ref, left_ref, right_ref, rel_ref,
    gh_high_ref, gh_low_ref, rgrad_ref, right_new_ref,
    left_t, right_t, rel_high_t, rel_low_t, rgrad, tgrad,
):
    n_left, width = left_ref.shape
    n_right, n_rel = right_ref.shape[0], rel_ref.shape[0]
    half = width // 2
    blocks = src_ref.shape[0]
    negs = neg_ref.shape[0] * neg_ref.shape[2]
    count = count_ref[0]
    eye = jnp.where(
        lax.broadcasted_iota(jnp.int32, (width, width), 0)
        == lax.broadcasted_iota(jnp.int32, (width, width), 1),
        1.0,
        0.0,
    ).astype(BF16)
    left_t[...] = mm_nt(eye, left_ref[...]).astype(BF16)
    right_t[...] = mm_nt(eye, right_ref[...]).astype(BF16)
    rel_high, rel_low = two_parts(rel_ref[...])
    rel_high_t[...] = mm_nt(eye, rel_high).astype(BF16)
    rel_low_t[...] = mm_nt(eye, rel_low).astype(BF16)
    seen = one_hot(n_right, neg_ref[0])
    for i in range(1, neg_ref.shape[0]):
        seen = seen + one_hot(n_right, neg_ref[i])
    times = jnp.sum(seen, axis=1, keepdims=True) * (1.0 / negs)
    rgrad[...] = jnp.zeros_like(rgrad)
    tgrad[...] = jnp.zeros_like(tgrad)

    def block(i, carry):
        ohs = one_hot(n_left, src_ref[i]).astype(BF16)
        ohk = one_hot(n_rel, kind_ref[i]).astype(BF16)
        ohd = one_hot(n_right, dst_ref[i]).astype(BF16)
        head = mm(left_t[...], ohs)
        tail = mm(right_t[...], ohd)
        rel = mm(rel_high_t[...], ohk) + mm(rel_low_t[...], ohk)
        hre, him = head[:half], head[half:]
        rre, rim = rel[:half], rel[half:]
        query = jnp.concatenate([hre * rre - him * rim, hre * rim + him * rre], axis=0)
        q_low = query.astype(BF16)
        pos = jnp.sum(query * tail, axis=0, keepdims=True)
        slot = i * EDGES + lax.broadcasted_iota(jnp.int32, (1, EDGES), 1)
        live = jnp.where(slot < count, 1.0, 0.0)
        c_pos = -jax.nn.sigmoid(-pos) * live
        scores = mm(right_ref[...], q_low)
        c_neg = (jax.nn.sigmoid(scores) * (times * live)).astype(BF16)
        g_query = mm(right_t[...], c_neg) + c_pos * tail
        gre, gim = g_query[:half], g_query[half:]
        grad_h = jnp.concatenate([gre * rre + gim * rim, -gre * rim + gim * rre], axis=0)
        grad_r = jnp.concatenate([gre * hre + gim * him, -gre * him + gim * hre], axis=0)
        gh_high_ref[i], gh_low_ref[i] = two_parts(grad_h)
        rgrad[...] += mm_nt(ohk, grad_r.astype(BF16))
        t_high, t_low = two_parts(c_pos * query)
        tgrad[...] += mm_nt(c_neg, q_low) + mm_nt(ohd, t_high) + mm_nt(ohd, t_low)
        return carry

    lax.fori_loop(0, blocks, block, 0)
    rgrad_ref[...] = rgrad[...].astype(BF16)
    right_new_ref[...] = (right_ref[...].astype(F32) - step_size * tgrad[...]).astype(BF16)


def left_kernel(src_ref, gh_high_ref, gh_low_ref, lgrad_ref):
    n_left, width = lgrad_ref.shape
    blocks = src_ref.shape[0]

    def rows(j, carry):
        start = pl.multiple_of(j * ROWS, ROWS)
        total = jnp.zeros((ROWS, width), F32)
        for i in range(blocks):
            hot = one_hot(ROWS, src_ref[i] - start).astype(BF16)
            total += mm_nt(hot, gh_high_ref[i]) + mm_nt(hot, gh_low_ref[i])
        lgrad_ref[pl.ds(start, ROWS), :] = total
        return carry

    lax.fori_loop(0, n_left // ROWS, rows, 0)


VMEM = pl.BlockSpec(memory_space=pltpu.VMEM)


def edge_grads(count, src, kind, dst, neg, left_blk, right_blk, relations, interpret=False):
    n_left, width = left_blk.shape
    n_right, n_rel, blocks = right_blk.shape[0], relations.shape[0], src.shape[0]
    return pl.pallas_call(
        edge_kernel,
        out_shape=(
            jax.ShapeDtypeStruct((blocks, width, EDGES), BF16),
            jax.ShapeDtypeStruct((blocks, width, EDGES), BF16),
            jax.ShapeDtypeStruct((n_rel, width), BF16),
            jax.ShapeDtypeStruct((n_right, width), BF16),
        ),
        in_specs=[pl.BlockSpec(memory_space=pltpu.SMEM)] + [VMEM] * 7,
        out_specs=(VMEM,) * 4,
        scratch_shapes=[
            pltpu.VMEM((width, n_left), BF16),
            pltpu.VMEM((width, n_right), BF16),
            pltpu.VMEM((width, n_rel), BF16),
            pltpu.VMEM((width, n_rel), BF16),
            pltpu.VMEM((n_rel, width), F32),
            pltpu.VMEM((n_right, width), F32),
        ],
        interpret=interpret,
        name="edges",
    )(count, src, kind, dst, neg, left_blk, right_blk, relations)


def left_sums(src, gh_high, gh_low, n_left, interpret=False):
    width = gh_high.shape[1]
    return pl.pallas_call(
        left_kernel,
        out_shape=jax.ShapeDtypeStruct((n_left, width), F32),
        in_specs=[VMEM] * 3,
        out_specs=VMEM,
        cost_estimate=pl.CostEstimate(
            flops=4 * n_left * src.size * width, transcendentals=0, bytes_accessed=8 * n_left * width
        ),
        interpret=interpret,
        name="leftrows",
    )(src, gh_high, gh_low)


def to_all(rows, axis):
    peers = lax.axis_size(axis)
    copies = jnp.broadcast_to(rows[None], (peers,) + rows.shape)
    return lax.all_to_all(copies, axis, 0, 0)


def shards(
    left_table, right_table, relations, source_ids, relation_ids, target_ids, negative_ids, edge_counts
):
    width = relations.shape[1]
    peers = lax.axis_size("right")
    mine = lax.axis_index("right")
    own_left = left_table.shape[0] // peers
    own_rel = relations.shape[0] // peers
    src, kind, dst, neg = (
        ids.reshape(-1, 1, EDGES) for ids in (source_ids, relation_ids, target_ids, negative_ids)
    )
    gh_high, gh_low, rel_grad, updated = edge_grads(
        edge_counts.reshape(1), src, kind, dst, neg, left_table, right_table[0], relations
    )
    moved = passed_along(updated, "right", 1)
    rel_got = lax.all_to_all(rel_grad.reshape(peers, own_rel, width), "right", 0, 0)
    left_grad = left_sums(src, gh_high, gh_low, left_table.shape[0])
    sent = left_grad.astype(jnp.float16).reshape(peers, own_left, width)
    rel_part = jnp.sum(rel_got.astype(F32), axis=0)
    left_got = lax.all_to_all(sent, "right", 0, 0)
    rel_parts = lax.all_gather(rel_part, "left", axis=0)
    rel_rows = lax.dynamic_slice_in_dim(relations, mine * own_rel, own_rel, 0)
    rel_rows = rel_rows - relation_step * jnp.sum(rel_parts, axis=0)
    left_rows = lax.dynamic_slice_in_dim(left_table, mine * own_left, own_left, 0)
    left_total = jnp.sum(left_got.astype(F32), axis=0)
    left_rows = (left_rows.astype(F32) - step_size * left_total).astype(BF16)
    squares = rel_rows * rel_rows
    code = (jnp.where(rel_rows < 0, -squares, squares) * squares).astype(BF16)
    out = to_all(jnp.concatenate([left_rows, code], axis=0), "right")
    left_next = out[:, :own_left].reshape(left_table.shape)
    code = out[:, own_left:].astype(F32)
    roots = jnp.sqrt(jnp.sqrt(jnp.abs(code)))
    relations_next = jnp.where(code < 0, -roots, roots).reshape(relations.shape)
    return (left_next, moved[None], relations_next)


def solution(mesh):
    return jax.shard_map(
        shards,
        mesh=mesh,
        in_specs=(
            P("left", None),
            P("left", "right", None),
            P(),
            P("left", "right", None),
            P("left", "right", None),
            P("left", "right", None),
            P("left", "right", None, None),
            P("left", "right"),
        ),
        out_specs=(P("left", None), P("left", "right", None), P()),
        check_vma=False,
    )
```

```python
import jax
import jax.numpy as jnp
import numpy as np
from jax import lax
from jax.experimental import pallas as pl
from jax.experimental.pallas import tpu as pltpu
from jax.sharding import PartitionSpec as P


step_size = 0.5
relation_step = 12.0
EDGES = 256
ROWS = 256
F32 = jnp.float32
BF16 = jnp.bfloat16


def passed_along(array, axis, by):
    peers = lax.axis_size(axis)
    return lax.ppermute(array, axis, [(i, (i + by) % peers) for i in range(peers)])


def mm(a, b):
    return lax.dot_general(a, b, (((1,), (0,)), ((), ())), preferred_element_type=F32)


def mm_nt(a, b):
    return lax.dot_general(a, b, (((1,), (1,)), ((), ())), preferred_element_type=F32)


def two_parts(x):
    high = x.astype(BF16)
    return high, (x - high.astype(F32)).astype(BF16)


def one_hot(rows, ids):
    return jnp.where(lax.broadcasted_iota(jnp.int32, (rows, ids.shape[1]), 0) == ids, 1.0, 0.0)


def edge_kernel(
    count_ref, src_ref, kind_ref, dst_ref, neg_ref, left_ref, right_ref, rel_ref,
    gh_high_ref, gh_low_ref, rgrad_ref, right_new_ref,
    left_t, right_t, rel_high_t, rel_low_t, rgrad, tgrad,
):
    n_left, width = left_ref.shape
    n_right, n_rel = right_ref.shape[0], rel_ref.shape[0]
    half = width // 2
    blocks = src_ref.shape[0]
    negs = neg_ref.shape[0] * neg_ref.shape[2]
    count = count_ref[0]
    eye = jnp.where(
        lax.broadcasted_iota(jnp.int32, (width, width), 0)
        == lax.broadcasted_iota(jnp.int32, (width, width), 1),
        1.0,
        0.0,
    ).astype(BF16)
    left_t[...] = mm_nt(eye, left_ref[...]).astype(BF16)
    right_t[...] = mm_nt(eye, right_ref[...]).astype(BF16)
    rel_high, rel_low = two_parts(rel_ref[...])
    rel_high_t[...] = mm_nt(eye, rel_high).astype(BF16)
    rel_low_t[...] = mm_nt(eye, rel_low).astype(BF16)
    seen = one_hot(n_right, neg_ref[0])
    for i in range(1, neg_ref.shape[0]):
        seen = seen + one_hot(n_right, neg_ref[i])
    times = jnp.sum(seen, axis=1, keepdims=True) * (1.0 / negs)
    rgrad[...] = jnp.zeros_like(rgrad)
    tgrad[...] = jnp.zeros_like(tgrad)

    def block(i, carry):
        ohs = one_hot(n_left, src_ref[i]).astype(BF16)
        ohk = one_hot(n_rel, kind_ref[i]).astype(BF16)
        ohd = one_hot(n_right, dst_ref[i]).astype(BF16)
        head = mm(left_t[...], ohs)
        tail = mm(right_t[...], ohd)
        rel = mm(rel_high_t[...], ohk) + mm(rel_low_t[...], ohk)
        hre, him = head[:half], head[half:]
        rre, rim = rel[:half], rel[half:]
        query = jnp.concatenate([hre * rre - him * rim, hre * rim + him * rre], axis=0)
        q_low = query.astype(BF16)
        pos = jnp.sum(query * tail, axis=0, keepdims=True)
        slot = i * EDGES + lax.broadcasted_iota(jnp.int32, (1, EDGES), 1)
        live = jnp.where(slot < count, 1.0, 0.0)
        c_pos = -jax.nn.sigmoid(-pos) * live
        scores = mm(right_ref[...], q_low)
        c_neg = (jax.nn.sigmoid(scores) * (times * live)).astype(BF16)
        g_query = mm(right_t[...], c_neg) + c_pos * tail
        gre, gim = g_query[:half], g_query[half:]
        grad_h = jnp.concatenate([gre * rre + gim * rim, -gre * rim + gim * rre], axis=0)
        grad_r = jnp.concatenate([gre * hre + gim * him, -gre * him + gim * hre], axis=0)
        gh_high_ref[i], gh_low_ref[i] = two_parts(grad_h)
        rgrad[...] += mm_nt(ohk, grad_r.astype(BF16))
        t_high, t_low = two_parts(c_pos * query)
        tgrad[...] += mm_nt(c_neg, q_low) + mm_nt(ohd, t_high) + mm_nt(ohd, t_low)
        return carry

    lax.fori_loop(0, blocks, block, 0)
    rgrad_ref[...] = rgrad[...].astype(BF16)
    right_new_ref[...] = (right_ref[...].astype(F32) - step_size * tgrad[...]).astype(BF16)


def left_kernel(src_ref, gh_high_ref, gh_low_ref, lgrad_ref):
    n_left, width = lgrad_ref.shape
    blocks = src_ref.shape[0]

    def rows(j, carry):
        start = pl.multiple_of(j * ROWS, ROWS)
        total = jnp.zeros((ROWS, width), F32)
        for i in range(blocks):
            hot = one_hot(ROWS, src_ref[i] - start).astype(BF16)
            total += mm_nt(hot, gh_high_ref[i]) + mm_nt(hot, gh_low_ref[i])
        lgrad_ref[pl.ds(start, ROWS), :] = total
        return carry

    lax.fori_loop(0, n_left // ROWS, rows, 0)


VMEM = pl.BlockSpec(memory_space=pltpu.VMEM)


def edge_grads(count, src, kind, dst, neg, left_blk, right_blk, relations, interpret=False):
    n_left, width = left_blk.shape
    n_right, n_rel, blocks = right_blk.shape[0], relations.shape[0], src.shape[0]
    return pl.pallas_call(
        edge_kernel,
        out_shape=(
            jax.ShapeDtypeStruct((blocks, width, EDGES), BF16),
            jax.ShapeDtypeStruct((blocks, width, EDGES), BF16),
            jax.ShapeDtypeStruct((n_rel, width), BF16),
            jax.ShapeDtypeStruct((n_right, width), BF16),
        ),
        in_specs=[pl.BlockSpec(memory_space=pltpu.SMEM)] + [VMEM] * 7,
        out_specs=(VMEM,) * 4,
        scratch_shapes=[
            pltpu.VMEM((width, n_left), BF16),
            pltpu.VMEM((width, n_right), BF16),
            pltpu.VMEM((width, n_rel), BF16),
            pltpu.VMEM((width, n_rel), BF16),
            pltpu.VMEM((n_rel, width), F32),
            pltpu.VMEM((n_right, width), F32),
        ],
        interpret=interpret,
        name="edges",
    )(count, src, kind, dst, neg, left_blk, right_blk, relations)


def left_sums(src, gh_high, gh_low, n_left, interpret=False):
    width = gh_high.shape[1]
    return pl.pallas_call(
        left_kernel,
        out_shape=jax.ShapeDtypeStruct((n_left, width), F32),
        in_specs=[VMEM] * 3,
        out_specs=VMEM,
        cost_estimate=pl.CostEstimate(
            flops=4 * n_left * src.size * width, transcendentals=0, bytes_accessed=8 * n_left * width
        ),
        interpret=interpret,
        name="leftrows",
    )(src, gh_high, gh_low)


def summed_over(part, axis, sizes):
    peers = np.arange(lax.axis_size(axis)).reshape(sizes)
    for dim in (0, 2, 1):
        groups = np.moveaxis(peers, dim, -1).reshape(-1, sizes[dim]).tolist()
        part = jnp.sum(lax.all_gather(part, axis, axis=0, axis_index_groups=groups), axis=0)
    return part


def to_all(rows, axis):
    peers = lax.axis_size(axis)
    copies = jnp.broadcast_to(rows[None], (peers,) + rows.shape)
    return lax.all_to_all(copies, axis, 0, 0)


def shards(
    left_table, right_table, relations, source_ids, relation_ids, target_ids, negative_ids, edge_counts
):
    width = relations.shape[1]
    peers = lax.axis_size("right")
    mine = lax.axis_index("right")
    own_left = left_table.shape[0] // peers
    own_rel = relations.shape[0] // peers
    src, kind, dst, neg = (
        ids.reshape(-1, 1, EDGES) for ids in (source_ids, relation_ids, target_ids, negative_ids)
    )
    gh_high, gh_low, rel_grad, updated = edge_grads(
        edge_counts.reshape(1), src, kind, dst, neg, left_table, right_table[0], relations
    )
    moved = passed_along(updated, "right", 1)
    rel_got = lax.all_to_all(rel_grad.reshape(peers, own_rel, width), "right", 0, 0)
    left_grad = left_sums(src, gh_high, gh_low, left_table.shape[0])
    sent = left_grad.astype(jnp.float16).reshape(peers, own_left, width)
    rel_part = jnp.sum(rel_got.astype(F32), axis=0)
    left_got = lax.all_to_all(sent, "right", 0, 0)
    rel_total = summed_over(rel_part, "left", (4, 2, 2))
    rel_rows = lax.dynamic_slice_in_dim(relations, mine * own_rel, own_rel, 0)
    rel_rows = rel_rows - relation_step * rel_total
    left_rows = lax.dynamic_slice_in_dim(left_table, mine * own_left, own_left, 0)
    left_total = jnp.sum(left_got.astype(F32), axis=0)
    left_rows = (left_rows.astype(F32) - step_size * left_total).astype(BF16)
    squares = rel_rows * rel_rows
    code = (jnp.where(rel_rows < 0, -squares, squares) * squares).astype(BF16)
    out = to_all(jnp.concatenate([left_rows, code], axis=0), "right")
    left_next = out[:, :own_left].reshape(left_table.shape)
    code = out[:, own_left:].astype(F32)
    roots = jnp.sqrt(jnp.sqrt(jnp.abs(code)))
    relations_next = jnp.where(code < 0, -roots, roots).reshape(relations.shape)
    return (left_next, moved[None], relations_next)


def solution(mesh):
    return jax.shard_map(
        shards,
        mesh=mesh,
        in_specs=(
            P("left", None),
            P("left", "right", None),
            P(),
            P("left", "right", None),
            P("left", "right", None),
            P("left", "right", None),
            P("left", "right", None, None),
            P("left", "right"),
        ),
        out_specs=(P("left", None), P("left", "right", None), P()),
        check_vma=False,
    )
```

```python
import jax
import jax.numpy as jnp
import numpy as np
from jax import lax
from jax.experimental import pallas as pl
from jax.experimental.pallas import tpu as pltpu
from jax.sharding import PartitionSpec as P


step_size = 0.5
relation_step = 12.0
EDGES = 1024
ROWS = 1024
F32 = jnp.float32
BF16 = jnp.bfloat16


def passed_along(array, axis, by):
    peers = lax.axis_size(axis)
    return lax.ppermute(array, axis, [(i, (i + by) % peers) for i in range(peers)])


def mm(a, b):
    return lax.dot_general(a, b, (((1,), (0,)), ((), ())), preferred_element_type=F32)


def mm_nt(a, b):
    return lax.dot_general(a, b, (((1,), (1,)), ((), ())), preferred_element_type=F32)


def two_parts(x):
    high = x.astype(BF16)
    return high, (x - high.astype(F32)).astype(BF16)


def one_hot(rows, ids):
    return jnp.where(lax.broadcasted_iota(jnp.int32, (rows, ids.shape[1]), 0) == ids, 1.0, 0.0)


def edge_kernel(
    count_ref, src_ref, kind_ref, dst_ref, neg_ref, left_ref, right_ref, rel_ref,
    gh_high_ref, gh_low_ref, rgrad_ref, right_new_ref,
    left_t, right_t, rel_high_t, rel_low_t, rgrad, tgrad,
):
    n_left, width = left_ref.shape
    n_right, n_rel = right_ref.shape[0], rel_ref.shape[0]
    half = width // 2
    blocks = src_ref.shape[0]
    negs = neg_ref.shape[0] * neg_ref.shape[2]
    count = count_ref[0]
    eye = jnp.where(
        lax.broadcasted_iota(jnp.int32, (width, width), 0)
        == lax.broadcasted_iota(jnp.int32, (width, width), 1),
        1.0,
        0.0,
    ).astype(BF16)
    left_t[...] = mm_nt(eye, left_ref[...]).astype(BF16)
    right_t[...] = mm_nt(eye, right_ref[...]).astype(BF16)
    rel_high, rel_low = two_parts(rel_ref[...])
    rel_high_t[...] = mm_nt(eye, rel_high).astype(BF16)
    rel_low_t[...] = mm_nt(eye, rel_low).astype(BF16)
    seen = one_hot(n_right, neg_ref[0])
    for i in range(1, neg_ref.shape[0]):
        seen = seen + one_hot(n_right, neg_ref[i])
    times = jnp.sum(seen, axis=1, keepdims=True) * (1.0 / negs)
    rgrad[...] = jnp.zeros_like(rgrad)
    tgrad[...] = jnp.zeros_like(tgrad)

    def block(i, carry):
        ohs = one_hot(n_left, src_ref[i]).astype(BF16)
        ohk = one_hot(n_rel, kind_ref[i]).astype(BF16)
        ohd = one_hot(n_right, dst_ref[i]).astype(BF16)
        head = mm(left_t[...], ohs)
        tail = mm(right_t[...], ohd)
        rel = mm(rel_high_t[...], ohk) + mm(rel_low_t[...], ohk)
        hre, him = head[:half], head[half:]
        rre, rim = rel[:half], rel[half:]
        query = jnp.concatenate([hre * rre - him * rim, hre * rim + him * rre], axis=0)
        q_low = query.astype(BF16)
        pos = jnp.sum(query * tail, axis=0, keepdims=True)
        slot = i * EDGES + lax.broadcasted_iota(jnp.int32, (1, EDGES), 1)
        live = jnp.where(slot < count, 1.0, 0.0)
        c_pos = -jax.nn.sigmoid(-pos) * live
        scores = mm(right_ref[...], q_low)
        c_neg = (jax.nn.sigmoid(scores) * (times * live)).astype(BF16)
        g_query = mm(right_t[...], c_neg) + c_pos * tail
        gre, gim = g_query[:half], g_query[half:]
        grad_h = jnp.concatenate([gre * rre + gim * rim, -gre * rim + gim * rre], axis=0)
        grad_r = jnp.concatenate([gre * hre + gim * him, -gre * him + gim * hre], axis=0)
        gh_high_ref[i], gh_low_ref[i] = two_parts(grad_h)
        rgrad[...] += mm_nt(ohk, grad_r.astype(BF16))
        t_high, t_low = two_parts(c_pos * query)
        tgrad[...] += mm_nt(c_neg, q_low) + mm_nt(ohd, t_high) + mm_nt(ohd, t_low)
        return carry

    lax.fori_loop(0, blocks, block, 0)
    rgrad_ref[...] = rgrad[...].astype(BF16)
    right_new_ref[...] = (right_ref[...].astype(F32) - step_size * tgrad[...]).astype(BF16)


def left_kernel(src_ref, gh_high_ref, gh_low_ref, lgrad_ref):
    n_left, width = lgrad_ref.shape
    blocks = src_ref.shape[0]

    def rows(j, carry):
        start = pl.multiple_of(j * ROWS, ROWS)
        total = jnp.zeros((ROWS, width), F32)
        for i in range(blocks):
            hot = one_hot(ROWS, src_ref[i] - start).astype(BF16)
            total += mm_nt(hot, gh_high_ref[i]) + mm_nt(hot, gh_low_ref[i])
        lgrad_ref[pl.ds(start, ROWS), :] = total
        return carry

    lax.fori_loop(0, n_left // ROWS, rows, 0)


VMEM = pl.BlockSpec(memory_space=pltpu.VMEM)


def edge_grads(count, src, kind, dst, neg, left_blk, right_blk, relations, interpret=False):
    n_left, width = left_blk.shape
    n_right, n_rel, blocks = right_blk.shape[0], relations.shape[0], src.shape[0]
    return pl.pallas_call(
        edge_kernel,
        out_shape=(
            jax.ShapeDtypeStruct((blocks, width, EDGES), BF16),
            jax.ShapeDtypeStruct((blocks, width, EDGES), BF16),
            jax.ShapeDtypeStruct((n_rel, width), BF16),
            jax.ShapeDtypeStruct((n_right, width), BF16),
        ),
        in_specs=[pl.BlockSpec(memory_space=pltpu.SMEM)] + [VMEM] * 7,
        out_specs=(VMEM,) * 4,
        scratch_shapes=[
            pltpu.VMEM((width, n_left), BF16),
            pltpu.VMEM((width, n_right), BF16),
            pltpu.VMEM((width, n_rel), BF16),
            pltpu.VMEM((width, n_rel), BF16),
            pltpu.VMEM((n_rel, width), F32),
            pltpu.VMEM((n_right, width), F32),
        ],
        interpret=interpret,
        name="edges",
    )(count, src, kind, dst, neg, left_blk, right_blk, relations)


def left_sums(src, gh_high, gh_low, n_left, interpret=False):
    width = gh_high.shape[1]
    return pl.pallas_call(
        left_kernel,
        out_shape=jax.ShapeDtypeStruct((n_left, width), F32),
        in_specs=[VMEM] * 3,
        out_specs=VMEM,
        cost_estimate=pl.CostEstimate(
            flops=4 * n_left * src.size * width, transcendentals=0, bytes_accessed=8 * n_left * width
        ),
        interpret=interpret,
        name="leftrows",
    )(src, gh_high, gh_low)


def summed_over(part, axis, sizes):
    peers = np.arange(lax.axis_size(axis)).reshape(sizes)
    for dim in (0, 2, 1):
        groups = np.moveaxis(peers, dim, -1).reshape(-1, sizes[dim]).tolist()
        part = jnp.sum(lax.all_gather(part, axis, axis=0, axis_index_groups=groups), axis=0)
    return part


def spread_kernel(total_ref, left_ref, code_ref, sent_ref, rows, done):
    own_left, own_rel = left_ref.shape[0], code_ref.shape[0]
    rows[:own_left] = (left_ref[...].astype(F32) - step_size * total_ref[...]).astype(BF16)
    rows[own_left : own_left + own_rel] = code_ref[...]
    copies = [pltpu.make_async_copy(rows, sent_ref.at[i], done.at[i]) for i in range(sent_ref.shape[0])]
    for copy in copies:
        copy.start()
    for copy in copies:
        copy.wait()


def for_all(total, left_rows, code, peers):
    shape = (left_rows.shape[0] + code.shape[0], left_rows.shape[1])
    return pl.pallas_call(
        spread_kernel,
        out_shape=jax.ShapeDtypeStruct((peers,) + shape, BF16),
        in_specs=[VMEM] * 3,
        out_specs=pl.BlockSpec(memory_space=pl.ANY),
        scratch_shapes=[pltpu.VMEM(shape, BF16), pltpu.SemaphoreType.DMA((peers,))],
        compiler_params=pltpu.CompilerParams(vmem_limit_bytes=4 * 2**20),
        name="spread",
    )(total, left_rows, code)


def settle_kernel(block_ref, out_ref, done):
    copy = pltpu.make_async_copy(block_ref, out_ref, done)
    copy.start()
    copy.wait()


def settled(block):
    return pl.pallas_call(
        settle_kernel,
        out_shape=jax.ShapeDtypeStruct(block.shape, block.dtype),
        in_specs=[VMEM],
        out_specs=pl.BlockSpec(memory_space=pl.ANY),
        scratch_shapes=[pltpu.SemaphoreType.DMA],
        compiler_params=pltpu.CompilerParams(vmem_limit_bytes=4 * 2**20),
        name="settle",
    )(block)


def finish_kernel(got_ref, left_next_ref, rel_next_ref, rel, done):
    own_left = left_next_ref.shape[1]
    left_copy = pltpu.make_async_copy(got_ref.at[:, :own_left, :], left_next_ref, done.at[0])
    left_copy.start()
    code = got_ref[:, own_left:, :].astype(F32)
    roots = jnp.sqrt(jnp.sqrt(jnp.abs(code)))
    rel[...] = jnp.where(code < 0, -roots, roots)
    rel_copy = pltpu.make_async_copy(rel, rel_next_ref, done.at[1])
    rel_copy.start()
    left_copy.wait()
    rel_copy.wait()


def finished(got, own_left):
    peers, rows, width = got.shape
    own_rel = rows - own_left
    return pl.pallas_call(
        finish_kernel,
        out_shape=(
            jax.ShapeDtypeStruct((peers, own_left, width), BF16),
            jax.ShapeDtypeStruct((peers, own_rel, width), F32),
        ),
        in_specs=[VMEM],
        out_specs=(pl.BlockSpec(memory_space=pl.ANY),) * 2,
        scratch_shapes=[pltpu.VMEM((peers, own_rel, width), F32), pltpu.SemaphoreType.DMA((2,))],
        compiler_params=pltpu.CompilerParams(vmem_limit_bytes=8 * 2**20),
        name="finish",
    )(got)


def shards(
    left_table, right_table, relations, source_ids, relation_ids, target_ids, negative_ids, edge_counts
):
    width = relations.shape[1]
    peers = lax.axis_size("right")
    mine = lax.axis_index("right")
    own_left = left_table.shape[0] // peers
    own_rel = relations.shape[0] // peers
    src, kind, dst, neg = (
        ids.reshape(-1, 1, EDGES) for ids in (source_ids, relation_ids, target_ids, negative_ids)
    )
    gh_high, gh_low, rel_grad, updated = edge_grads(
        edge_counts.reshape(1), src, kind, dst, neg, left_table, right_table[0], relations
    )
    moved = passed_along(updated[None], "right", 1)
    rel_got = lax.all_to_all(rel_grad.reshape(peers, own_rel, width), "right", 0, 0)
    left_grad = left_sums(src, gh_high, gh_low, left_table.shape[0])
    sent = left_grad.astype(jnp.float16).reshape(peers, own_left, width)
    rel_part = jnp.sum(rel_got.astype(F32), axis=0)
    left_got = lax.all_to_all(sent, "right", 0, 0)
    rel_total = summed_over(rel_part, "left", (4, 2, 2))
    rel_rows = lax.dynamic_slice_in_dim(relations, mine * own_rel, own_rel, 0)
    rel_rows = rel_rows - relation_step * rel_total
    left_rows = lax.dynamic_slice_in_dim(left_table, mine * own_left, own_left, 0)
    left_total = jnp.sum(left_got.astype(F32), axis=0)
    squares = rel_rows * rel_rows
    code = (jnp.where(rel_rows < 0, -squares, squares) * squares).astype(BF16)
    got = lax.all_to_all(for_all(left_total, left_rows, code, peers), "right", 0, 0)
    moved = settled(moved)
    left_next, relations_next = finished(got, own_left)
    return (left_next.reshape(left_table.shape), moved, relations_next.reshape(relations.shape))


def solution(mesh):
    return jax.shard_map(
        shards,
        mesh=mesh,
        in_specs=(
            P("left", None),
            P("left", "right", None),
            P(),
            P("left", "right", None),
            P("left", "right", None),
            P("left", "right", None),
            P("left", "right", None, None),
            P("left", "right"),
        ),
        out_specs=(P("left", None), P("left", "right", None), P()),
        check_vma=False,
    )
```

```python
import jax
import jax.numpy as jnp
import numpy as np
from jax import lax
from jax.experimental import pallas as pl
from jax.experimental.pallas import tpu as pltpu
from jax.sharding import PartitionSpec as P


step_size = 0.5
relation_step = 12.0
EDGES = 1024
ROWS = 1024
F32 = jnp.float32
BF16 = jnp.bfloat16


def passed_along(array, axis, by):
    peers = lax.axis_size(axis)
    return lax.ppermute(array, axis, [(i, (i + by) % peers) for i in range(peers)])


def mm(a, b):
    return lax.dot_general(a, b, (((1,), (0,)), ((), ())), preferred_element_type=F32)


def mm_nt(a, b):
    return lax.dot_general(a, b, (((1,), (1,)), ((), ())), preferred_element_type=F32)


def mm_tn(a, b):
    return lax.dot_general(a, b, (((0,), (0,)), ((), ())), preferred_element_type=F32)


def two_parts(x):
    high = x.astype(BF16)
    return high, (x - high.astype(F32)).astype(BF16)


def one_hot(rows, ids):
    places = lax.broadcasted_iota(jnp.int32, (rows, ids.shape[1]), 0)
    return jnp.where(places.astype(jnp.int16) == ids.astype(jnp.int16), BF16(1), BF16(0))


def edge_kernel(
    count_ref, src_ref, kind_ref, dst_ref, neg_ref, left_ref, right_ref, rel_ref,
    gh_high_ref, gh_low_ref, rgrad_ref, right_new_ref,
    right_t, rgrad, tgrad,
):
    n_left, width = left_ref.shape
    n_right, n_rel = right_ref.shape[0], rel_ref.shape[0]
    half = width // 2
    blocks = src_ref.shape[0]
    negs = neg_ref.shape[0] * neg_ref.shape[2]
    count = count_ref[...]
    eye = jnp.where(
        lax.broadcasted_iota(jnp.int32, (width, width), 0)
        == lax.broadcasted_iota(jnp.int32, (width, width), 1),
        1.0,
        0.0,
    ).astype(BF16)
    right_t[...] = mm_nt(eye, right_ref[...]).astype(BF16)
    rel_high, rel_low = two_parts(rel_ref[...])
    seen = one_hot(n_right, neg_ref[0]).astype(F32)
    for i in range(1, neg_ref.shape[0]):
        seen = seen + one_hot(n_right, neg_ref[i]).astype(F32)
    times = jnp.sum(seen, axis=1, keepdims=True) * (1.0 / negs)
    rgrad[...] = jnp.zeros_like(rgrad)
    tgrad[...] = jnp.zeros_like(tgrad)

    def block(i, carry):
        ohs = one_hot(n_left, src_ref[i])
        ohk = one_hot(n_rel, kind_ref[i])
        ohd = one_hot(n_right, dst_ref[i])
        head = mm_tn(left_ref[...], ohs)
        tail = mm(right_t[...], ohd)
        rel = mm_tn(rel_high, ohk) + mm_tn(rel_low, ohk)
        hre, him = head[:half], head[half:]
        rre, rim = rel[:half], rel[half:]
        query = jnp.concatenate([hre * rre - him * rim, hre * rim + him * rre], axis=0)
        q_low = query.astype(BF16)
        pos = jnp.sum(query * tail, axis=0, keepdims=True)
        slot = i * EDGES + lax.broadcasted_iota(jnp.int32, (1, EDGES), 1)
        live = jnp.where(slot < count, 1.0, 0.0)
        c_pos = -jax.nn.sigmoid(-pos) * live
        scores = mm(right_ref[...], q_low)
        c_neg = (jax.nn.sigmoid(scores) * (times * live)).astype(BF16)
        g_query = mm(right_t[...], c_neg) + c_pos * tail
        gre, gim = g_query[:half], g_query[half:]
        grad_h = jnp.concatenate([gre * rre + gim * rim, -gre * rim + gim * rre], axis=0)
        grad_r = jnp.concatenate([gre * hre + gim * him, -gre * him + gim * hre], axis=0)
        gh_high_ref[i], gh_low_ref[i] = two_parts(grad_h)
        rgrad[...] += mm_nt(ohk, grad_r.astype(BF16))
        t_high, t_low = two_parts(c_pos * query)
        tgrad[...] += mm_nt(c_neg, q_low) + mm_nt(ohd, t_high) + mm_nt(ohd, t_low)
        return carry

    lax.fori_loop(0, blocks, block, 0)
    rgrad_ref[...] = rgrad[...].astype(BF16)
    right_new_ref[...] = (right_ref[...].astype(F32) - step_size * tgrad[...]).astype(BF16)


def left_kernel(src_ref, gh_high_ref, gh_low_ref, lgrad_ref):
    n_left, width = lgrad_ref.shape
    blocks = src_ref.shape[0]

    def rows(j, carry):
        start = pl.multiple_of(j * ROWS, ROWS)
        total = jnp.zeros((ROWS, width), F32)
        for i in range(blocks):
            hot = one_hot(ROWS, src_ref[i] - start)
            total += mm_nt(hot, gh_high_ref[i]) + mm_nt(hot, gh_low_ref[i])
        lgrad_ref[pl.ds(start, ROWS), :] = total
        return carry

    lax.fori_loop(0, n_left // ROWS, rows, 0)


VMEM = pl.BlockSpec(memory_space=pltpu.VMEM)


def edge_grads(count, src, kind, dst, neg, left_blk, right_blk, relations, interpret=False):
    _, width = left_blk.shape
    n_right, n_rel, blocks = right_blk.shape[0], relations.shape[0], src.shape[0]
    return pl.pallas_call(
        edge_kernel,
        out_shape=(
            jax.ShapeDtypeStruct((blocks, width, EDGES), BF16),
            jax.ShapeDtypeStruct((blocks, width, EDGES), BF16),
            jax.ShapeDtypeStruct((n_rel, width), BF16),
            jax.ShapeDtypeStruct((n_right, width), BF16),
        ),
        in_specs=[VMEM] * 8,
        out_specs=(VMEM,) * 4,
        scratch_shapes=[
            pltpu.VMEM((width, n_right), BF16),
            pltpu.VMEM((n_rel, width), F32),
            pltpu.VMEM((n_right, width), F32),
        ],
        interpret=interpret,
        name="edges",
    )(count, src, kind, dst, neg, left_blk, right_blk, relations)


def left_sums(src, gh_high, gh_low, n_left, interpret=False):
    width = gh_high.shape[1]
    return pl.pallas_call(
        left_kernel,
        out_shape=jax.ShapeDtypeStruct((n_left, width), F32),
        in_specs=[VMEM] * 3,
        out_specs=VMEM,
        cost_estimate=pl.CostEstimate(
            flops=4 * n_left * src.size * width, transcendentals=0, bytes_accessed=8 * n_left * width
        ),
        interpret=interpret,
        name="leftrows",
    )(src, gh_high, gh_low)


def summed_over(part, axis, sizes):
    peers = np.arange(lax.axis_size(axis)).reshape(sizes)
    for dim in (0, 2, 1):
        groups = np.moveaxis(peers, dim, -1).reshape(-1, sizes[dim]).tolist()
        part = jnp.sum(lax.all_gather(part, axis, axis=0, axis_index_groups=groups), axis=0)
    return part


def spread_kernel(total_ref, left_ref, code_ref, sent_ref, rows, done):
    own_left, own_rel = left_ref.shape[0], code_ref.shape[0]
    rows[:own_left] = (left_ref[...].astype(F32) - step_size * total_ref[...]).astype(BF16)
    rows[own_left : own_left + own_rel] = code_ref[...]
    copies = [pltpu.make_async_copy(rows, sent_ref.at[i], done.at[i]) for i in range(sent_ref.shape[0])]
    for copy in copies:
        copy.start()
    for copy in copies:
        copy.wait()


def for_all(total, left_rows, code, peers):
    shape = (left_rows.shape[0] + code.shape[0], left_rows.shape[1])
    return pl.pallas_call(
        spread_kernel,
        out_shape=jax.ShapeDtypeStruct((peers,) + shape, BF16),
        in_specs=[VMEM] * 3,
        out_specs=pl.BlockSpec(memory_space=pl.ANY),
        scratch_shapes=[pltpu.VMEM(shape, BF16), pltpu.SemaphoreType.DMA((peers,))],
        compiler_params=pltpu.CompilerParams(vmem_limit_bytes=4 * 2**20),
        name="spread",
    )(total, left_rows, code)


def settle_kernel(block_ref, out_ref, done):
    copy = pltpu.make_async_copy(block_ref, out_ref, done)
    copy.start()
    copy.wait()


def settled(block):
    return pl.pallas_call(
        settle_kernel,
        out_shape=jax.ShapeDtypeStruct(block.shape, block.dtype),
        in_specs=[VMEM],
        out_specs=pl.BlockSpec(memory_space=pl.ANY),
        scratch_shapes=[pltpu.SemaphoreType.DMA],
        compiler_params=pltpu.CompilerParams(vmem_limit_bytes=4 * 2**20),
        name="settle",
    )(block)


def finish_kernel(got_ref, left_next_ref, rel_next_ref, rel, done):
    own_left = left_next_ref.shape[1]
    left_copy = pltpu.make_async_copy(got_ref.at[:, :own_left, :], left_next_ref, done.at[0])
    left_copy.start()
    code = got_ref[:, own_left:, :].astype(F32)
    roots = jnp.sqrt(jnp.sqrt(jnp.abs(code)))
    rel[...] = jnp.where(code < 0, -roots, roots)
    rel_copy = pltpu.make_async_copy(rel, rel_next_ref, done.at[1])
    rel_copy.start()
    left_copy.wait()
    rel_copy.wait()


def finished(got, own_left):
    peers, rows, width = got.shape
    own_rel = rows - own_left
    return pl.pallas_call(
        finish_kernel,
        out_shape=(
            jax.ShapeDtypeStruct((peers, own_left, width), BF16),
            jax.ShapeDtypeStruct((peers, own_rel, width), F32),
        ),
        in_specs=[VMEM],
        out_specs=(pl.BlockSpec(memory_space=pl.ANY),) * 2,
        scratch_shapes=[pltpu.VMEM((peers, own_rel, width), F32), pltpu.SemaphoreType.DMA((2,))],
        compiler_params=pltpu.CompilerParams(vmem_limit_bytes=8 * 2**20),
        name="finish",
    )(got)


def shards(
    left_table, right_table, relations, source_ids, relation_ids, target_ids, negative_ids, edge_counts
):
    width = relations.shape[1]
    peers = lax.axis_size("right")
    mine = lax.axis_index("right")
    own_left = left_table.shape[0] // peers
    own_rel = relations.shape[0] // peers
    src, kind, dst, neg = (
        ids.reshape(-1, 1, EDGES) for ids in (source_ids, relation_ids, target_ids, negative_ids)
    )
    gh_high, gh_low, rel_grad, updated = edge_grads(
        edge_counts, src, kind, dst, neg, left_table, right_table[0], relations
    )
    moved = passed_along(updated[None], "right", 1)
    rel_got = lax.all_to_all(rel_grad.reshape(peers, own_rel, width), "right", 0, 0)
    left_grad = left_sums(src, gh_high, gh_low, left_table.shape[0])
    sent = left_grad.astype(jnp.float16).reshape(peers, own_left, width)
    rel_part = jnp.sum(rel_got.astype(F32), axis=0)
    left_got = lax.all_to_all(sent, "right", 0, 0)
    rel_total = summed_over(rel_part, "left", (4, 2, 2))
    rel_rows = lax.dynamic_slice_in_dim(relations, mine * own_rel, own_rel, 0)
    rel_rows = rel_rows - relation_step * rel_total
    left_rows = lax.dynamic_slice_in_dim(left_table, mine * own_left, own_left, 0)
    left_total = jnp.sum(left_got.astype(F32), axis=0)
    squares = rel_rows * rel_rows
    code = (jnp.where(rel_rows < 0, -squares, squares) * squares).astype(BF16)
    got = lax.all_to_all(for_all(left_total, left_rows, code, peers), "right", 0, 0)
    moved = settled(moved)
    left_next, relations_next = finished(got, own_left)
    return (left_next.reshape(left_table.shape), moved, relations_next.reshape(relations.shape))


def solution(mesh):
    return jax.shard_map(
        shards,
        mesh=mesh,
        in_specs=(
            P("left", None),
            P("left", "right", None),
            P(),
            P("left", "right", None),
            P("left", "right", None),
            P("left", "right", None),
            P("left", "right", None, None),
            P("left", "right"),
        ),
        out_specs=(P("left", None), P("left", "right", None), P()),
        check_vma=False,
    )
```

```python
import jax
import jax.numpy as jnp
import numpy as np
from jax import lax
from jax.experimental import pallas as pl
from jax.experimental.pallas import tpu as pltpu
from jax.sharding import PartitionSpec as P


step_size = 0.5
relation_step = 12.0
EDGES = 1024
ROWS = 1024
F32 = jnp.float32
BF16 = jnp.bfloat16


def passed_along(array, axis, by):
    peers = lax.axis_size(axis)
    return lax.ppermute(array, axis, [(i, (i + by) % peers) for i in range(peers)])


def mm(a, b):
    return lax.dot_general(a, b, (((1,), (0,)), ((), ())), preferred_element_type=F32)


def mm_nt(a, b):
    return lax.dot_general(a, b, (((1,), (1,)), ((), ())), preferred_element_type=F32)


def mm_tn(a, b):
    return lax.dot_general(a, b, (((0,), (0,)), ((), ())), preferred_element_type=F32)


def two_parts(x):
    high = x.astype(BF16)
    return high, (x - high.astype(F32)).astype(BF16)


def one_hot(rows, ids):
    places = lax.broadcasted_iota(jnp.int32, (rows, ids.shape[1]), 0)
    return jnp.where(places.astype(jnp.int16) == ids.astype(jnp.int16), BF16(1), BF16(0))


def edge_kernel(
    count_ref, src_ref, kind_ref, dst_ref, neg_ref, left_ref, right_ref, rel_ref,
    gh_high_ref, gh_low_ref, rgrad_ref, right_new_ref, own_ref,
    right_t, rgrad, tgrad,
):
    n_left, width = left_ref.shape
    n_right, n_rel = right_ref.shape[0], rel_ref.shape[0]
    half = width // 2
    blocks = src_ref.shape[0]
    negs = neg_ref.shape[0] * neg_ref.shape[2]
    count = count_ref[...]
    eye = jnp.where(
        lax.broadcasted_iota(jnp.int32, (width, width), 0)
        == lax.broadcasted_iota(jnp.int32, (width, width), 1),
        1.0,
        0.0,
    ).astype(BF16)
    right_t[...] = mm_nt(eye, right_ref[...]).astype(BF16)
    rel_high, rel_low = two_parts(rel_ref[...])
    seen = one_hot(n_right, neg_ref[0]).astype(F32)
    for i in range(1, neg_ref.shape[0]):
        seen = seen + one_hot(n_right, neg_ref[i]).astype(F32)
    times = jnp.sum(seen, axis=1, keepdims=True) * (1.0 / negs)
    rgrad[...] = jnp.zeros_like(rgrad)
    tgrad[...] = jnp.zeros_like(tgrad)

    def block(i, carry):
        ohs = one_hot(n_left, src_ref[i])
        ohk = one_hot(n_rel, kind_ref[i])
        ohd = one_hot(n_right, dst_ref[i])
        head = mm_tn(left_ref[...], ohs)
        tail = mm(right_t[...], ohd)
        rel = mm_tn(rel_high, ohk) + mm_tn(rel_low, ohk)
        hre, him = head[:half], head[half:]
        rre, rim = rel[:half], rel[half:]
        query = jnp.concatenate([hre * rre - him * rim, hre * rim + him * rre], axis=0)
        q_low = query.astype(BF16)
        pos = jnp.sum(query * tail, axis=0, keepdims=True)
        slot = i * EDGES + lax.broadcasted_iota(jnp.int32, (1, EDGES), 1)
        live = jnp.where(slot < count, 1.0, 0.0)
        c_pos = -jax.nn.sigmoid(-pos) * live
        scores = mm(right_ref[...], q_low)
        c_neg = (jax.nn.sigmoid(scores) * (times * live)).astype(BF16)
        g_query = mm(right_t[...], c_neg) + c_pos * tail
        gre, gim = g_query[:half], g_query[half:]
        grad_h = jnp.concatenate([gre * rre + gim * rim, -gre * rim + gim * rre], axis=0)
        grad_r = jnp.concatenate([gre * hre + gim * him, -gre * him + gim * hre], axis=0)
        gh_high_ref[i], gh_low_ref[i] = two_parts(grad_h)
        rgrad[...] += mm_nt(ohk, grad_r.astype(BF16))
        t_high, t_low = two_parts(c_pos * query)
        tgrad[...] += mm_nt(c_neg, q_low) + mm_nt(ohd, t_high) + mm_nt(ohd, t_low)
        return carry

    lax.fori_loop(0, blocks, block, 0)
    rgrad_ref[...] = rgrad[...].astype(BF16)
    right_new_ref[...] = (right_ref[...].astype(F32) - step_size * tgrad[...]).astype(BF16)
    own = own_ref.shape[0]
    own_ref[...] = left_ref[pl.ds(pl.multiple_of(lax.axis_index("right") * own, own), own), :]


def left_kernel(src_ref, gh_high_ref, gh_low_ref, lgrad_ref):
    n_left, width = lgrad_ref.shape
    blocks = src_ref.shape[0]

    def rows(j, carry):
        start = pl.multiple_of(j * ROWS, ROWS)
        total = jnp.zeros((ROWS, width), F32)
        for i in range(blocks):
            hot = one_hot(ROWS, src_ref[i] - start)
            total += mm_nt(hot, gh_high_ref[i]) + mm_nt(hot, gh_low_ref[i])
        lgrad_ref[pl.ds(start, ROWS), :] = total
        return carry

    lax.fori_loop(0, n_left // ROWS, rows, 0)


VMEM = pl.BlockSpec(memory_space=pltpu.VMEM)


def edge_grads(own_left, count, src, kind, dst, neg, left_blk, right_blk, relations, interpret=False):
    _, width = left_blk.shape
    n_right, n_rel, blocks = right_blk.shape[0], relations.shape[0], src.shape[0]
    return pl.pallas_call(
        edge_kernel,
        out_shape=(
            jax.ShapeDtypeStruct((blocks, width, EDGES), BF16),
            jax.ShapeDtypeStruct((blocks, width, EDGES), BF16),
            jax.ShapeDtypeStruct((n_rel, width), BF16),
            jax.ShapeDtypeStruct((n_right, width), BF16),
            jax.ShapeDtypeStruct((own_left, width), BF16),
        ),
        in_specs=[VMEM] * 8,
        out_specs=(VMEM,) * 5,
        scratch_shapes=[
            pltpu.VMEM((width, n_right), BF16),
            pltpu.VMEM((n_rel, width), F32),
            pltpu.VMEM((n_right, width), F32),
        ],
        interpret=interpret,
        name="edges",
    )(count, src, kind, dst, neg, left_blk, right_blk, relations)


def left_sums(src, gh_high, gh_low, n_left, interpret=False):
    width = gh_high.shape[1]
    return pl.pallas_call(
        left_kernel,
        out_shape=jax.ShapeDtypeStruct((n_left, width), F32),
        in_specs=[VMEM] * 3,
        out_specs=VMEM,
        cost_estimate=pl.CostEstimate(
            flops=4 * n_left * src.size * width, transcendentals=0, bytes_accessed=8 * n_left * width
        ),
        compiler_params=pltpu.CompilerParams(vmem_limit_bytes=32 * 2**20),
        interpret=interpret,
        name="leftrows",
    )(*(pltpu.with_memory_space_constraint(a, pltpu.HBM) for a in (src, gh_high, gh_low)))


def summed_over(part, axis, sizes):
    peers = np.arange(lax.axis_size(axis)).reshape(sizes)
    for dim in (1, 0, 3, 2):
        groups = np.moveaxis(peers, dim, -1).reshape(-1, sizes[dim]).tolist()
        part = jnp.sum(lax.all_gather(part, axis, axis=0, axis_index_groups=groups), axis=0)
    return part


def spread_kernel(total_ref, left_ref, code_ref, sent_ref, rows, done):
    own_left, own_rel = left_ref.shape[0], code_ref.shape[0]
    rows[:own_left] = (left_ref[...].astype(F32) - step_size * total_ref[...]).astype(BF16)
    rows[own_left : own_left + own_rel] = code_ref[...]
    copies = [pltpu.make_async_copy(rows, sent_ref.at[i], done.at[i]) for i in range(sent_ref.shape[0])]
    for copy in copies:
        copy.start()
    for copy in copies:
        copy.wait()


def for_all(total, left_rows, code, peers):
    shape = (left_rows.shape[0] + code.shape[0], left_rows.shape[1])
    return pl.pallas_call(
        spread_kernel,
        out_shape=jax.ShapeDtypeStruct((peers,) + shape, BF16),
        in_specs=[VMEM] * 3,
        out_specs=pl.BlockSpec(memory_space=pl.ANY),
        scratch_shapes=[pltpu.VMEM(shape, BF16), pltpu.SemaphoreType.DMA((peers,))],
        compiler_params=pltpu.CompilerParams(vmem_limit_bytes=4 * 2**20),
        name="spread",
    )(total, left_rows, code)


def settle_kernel(block_ref, out_ref, done):
    copy = pltpu.make_async_copy(block_ref, out_ref, done)
    copy.start()
    copy.wait()


def settled(block):
    return pl.pallas_call(
        settle_kernel,
        out_shape=jax.ShapeDtypeStruct(block.shape, block.dtype),
        in_specs=[VMEM],
        out_specs=pl.BlockSpec(memory_space=pl.ANY),
        scratch_shapes=[pltpu.SemaphoreType.DMA],
        compiler_params=pltpu.CompilerParams(vmem_limit_bytes=4 * 2**20),
        name="settle",
    )(block)


def finish_kernel(got_ref, left_next_ref, rel_next_ref, rel, done):
    own_left = left_next_ref.shape[1]
    left_copy = pltpu.make_async_copy(got_ref.at[:, :own_left, :], left_next_ref, done.at[0])
    left_copy.start()
    code = got_ref[:, own_left:, :].astype(F32)
    roots = jnp.sqrt(jnp.sqrt(jnp.abs(code)))
    rel[...] = jnp.where(code < 0, -roots, roots)
    rel_copy = pltpu.make_async_copy(rel, rel_next_ref, done.at[1])
    rel_copy.start()
    left_copy.wait()
    rel_copy.wait()


def finished(got, own_left):
    peers, rows, width = got.shape
    own_rel = rows - own_left
    return pl.pallas_call(
        finish_kernel,
        out_shape=(
            jax.ShapeDtypeStruct((peers, own_left, width), BF16),
            jax.ShapeDtypeStruct((peers, own_rel, width), F32),
        ),
        in_specs=[VMEM],
        out_specs=(pl.BlockSpec(memory_space=pl.ANY),) * 2,
        scratch_shapes=[pltpu.VMEM((peers, own_rel, width), F32), pltpu.SemaphoreType.DMA((2,))],
        compiler_params=pltpu.CompilerParams(vmem_limit_bytes=8 * 2**20),
        name="finish",
    )(got)


def shards(
    left_table, right_table, relations, source_ids, relation_ids, target_ids, negative_ids, edge_counts
):
    width = relations.shape[1]
    peers = lax.axis_size("right")
    mine = lax.axis_index("right")
    own_left = left_table.shape[0] // peers
    own_rel = relations.shape[0] // peers
    src, kind, dst, neg = (
        ids.reshape(-1, 1, EDGES) for ids in (source_ids, relation_ids, target_ids, negative_ids)
    )
    gh_high, gh_low, rel_grad, updated, left_rows = edge_grads(
        own_left, edge_counts, src, kind, dst, neg, left_table, right_table[0], relations
    )
    moved = passed_along(updated[None], "right", 1)
    rel_got = lax.all_to_all(rel_grad.reshape(peers, own_rel, width), "right", 0, 0)
    left_grad = left_sums(src, gh_high, gh_low, left_table.shape[0])
    sent = left_grad.astype(jnp.float16).reshape(peers, own_left, width)
    rel_part = jnp.sum(rel_got.astype(F32), axis=0)
    left_got = lax.all_to_all(sent, "right", 0, 0)
    rel_total = summed_over(rel_part, "left", (2, 2, 2, 2))
    rel_rows = lax.dynamic_slice_in_dim(relations, mine * own_rel, own_rel, 0)
    rel_rows = rel_rows - relation_step * rel_total
    left_total = jnp.sum(left_got.astype(F32), axis=0)
    squares = rel_rows * rel_rows
    code = (jnp.where(rel_rows < 0, -squares, squares) * squares).astype(BF16)
    got = lax.all_to_all(for_all(left_total, left_rows, code, peers), "right", 0, 0)
    moved = settled(moved)
    left_next, relations_next = finished(got, own_left)
    return (left_next.reshape(left_table.shape), moved, relations_next.reshape(relations.shape))


def solution(mesh):
    return jax.shard_map(
        shards,
        mesh=mesh,
        in_specs=(
            P("left", None),
            P("left", "right", None),
            P(),
            P("left", "right", None),
            P("left", "right", None),
            P("left", "right", None),
            P("left", "right", None, None),
            P("left", "right"),
        ),
        out_specs=(P("left", None), P("left", "right", None), P()),
        check_vma=False,
    )
```

```python
import jax
import jax.numpy as jnp
import numpy as np
from jax import lax
from jax.experimental import pallas as pl
from jax.experimental.pallas import tpu as pltpu
from jax.sharding import PartitionSpec as P


step_size = 0.5
relation_step = 12.0
EDGES = 1024
ROWS = 1024
F32 = jnp.float32
BF16 = jnp.bfloat16


def passed_along(array, axis, by):
    peers = lax.axis_size(axis)
    return lax.ppermute(array, axis, [(i, (i + by) % peers) for i in range(peers)])


def mm(a, b):
    return lax.dot_general(a, b, (((1,), (0,)), ((), ())), preferred_element_type=F32)


def mm_nt(a, b):
    return lax.dot_general(a, b, (((1,), (1,)), ((), ())), preferred_element_type=F32)


def mm_tn(a, b):
    return lax.dot_general(a, b, (((0,), (0,)), ((), ())), preferred_element_type=F32)


def two_parts(x):
    high = x.astype(BF16)
    return high, (x - high.astype(F32)).astype(BF16)


def one_hot(rows, ids):
    places = lax.broadcasted_iota(jnp.int32, (rows, ids.shape[1]), 0)
    return jnp.where(places.astype(jnp.int16) == ids.astype(jnp.int16), BF16(1), BF16(0))


def edge_kernel(
    count_ref, src_ref, kind_ref, dst_ref, neg_ref, left_ref, right_ref, rel_ref,
    gh_high_ref, gh_low_ref, rgrad_ref, right_new_ref, own_ref,
    right_t, rgrad, tgrad,
):
    n_left, width = left_ref.shape
    n_right, n_rel = right_ref.shape[0], rel_ref.shape[0]
    half = width // 2
    blocks = src_ref.shape[0]
    negs = neg_ref.shape[0] * neg_ref.shape[2]
    count = count_ref[...]
    eye = jnp.where(
        lax.broadcasted_iota(jnp.int32, (width, width), 0)
        == lax.broadcasted_iota(jnp.int32, (width, width), 1),
        1.0,
        0.0,
    ).astype(BF16)
    right_t[...] = mm_nt(eye, right_ref[...]).astype(BF16)
    rel_high, rel_low = two_parts(rel_ref[...])
    seen = one_hot(n_right, neg_ref[0]).astype(F32)
    for i in range(1, neg_ref.shape[0]):
        seen = seen + one_hot(n_right, neg_ref[i]).astype(F32)
    times = jnp.sum(seen, axis=1, keepdims=True) * (1.0 / negs)
    rgrad[...] = jnp.zeros_like(rgrad)
    tgrad[...] = jnp.zeros_like(tgrad)

    def block(i, carry):
        ohs = one_hot(n_left, src_ref[i])
        ohk = one_hot(n_rel, kind_ref[i])
        ohd = one_hot(n_right, dst_ref[i])
        head = mm_tn(left_ref[...], ohs)
        tail = mm(right_t[...], ohd)
        rel = mm_tn(rel_high, ohk) + mm_tn(rel_low, ohk)
        hre, him = head[:half], head[half:]
        rre, rim = rel[:half], rel[half:]
        query = jnp.concatenate([hre * rre - him * rim, hre * rim + him * rre], axis=0)
        q_low = query.astype(BF16)
        pos = jnp.sum(query * tail, axis=0, keepdims=True)
        slot = i * EDGES + lax.broadcasted_iota(jnp.int32, (1, EDGES), 1)
        live = jnp.where(slot < count, 1.0, 0.0)
        c_pos = -jax.nn.sigmoid(-pos) * live
        scores = mm(right_ref[...], q_low)
        c_neg = (jax.nn.sigmoid(scores) * (times * live)).astype(BF16)
        g_query = mm(right_t[...], c_neg) + c_pos * tail
        gre, gim = g_query[:half], g_query[half:]
        grad_h = jnp.concatenate([gre * rre + gim * rim, -gre * rim + gim * rre], axis=0)
        grad_r = jnp.concatenate([gre * hre + gim * him, -gre * him + gim * hre], axis=0)
        gh_high_ref[i], gh_low_ref[i] = two_parts(grad_h)
        rgrad[...] += mm_nt(ohk, grad_r.astype(BF16))
        t_high, t_low = two_parts(c_pos * query)
        tgrad[...] += mm_nt(c_neg, q_low) + mm_nt(ohd, t_high) + mm_nt(ohd, t_low)
        return carry

    lax.fori_loop(0, blocks, block, 0)
    rgrad_ref[...] = rgrad[...].astype(BF16)
    right_new_ref[...] = (right_ref[...].astype(F32) - step_size * tgrad[...]).astype(BF16)
    own = own_ref.shape[0]
    own_ref[...] = left_ref[pl.ds(pl.multiple_of(lax.axis_index("right") * own, own), own), :]


def left_kernel(src_ref, gh_high_ref, gh_low_ref, lgrad_ref):
    n_left, width = lgrad_ref.shape
    blocks = src_ref.shape[0]

    def rows(j, carry):
        start = pl.multiple_of(j * ROWS, ROWS)
        total = jnp.zeros((ROWS, width), F32)
        for i in range(blocks):
            hot = one_hot(ROWS, src_ref[i] - start)
            total += mm_nt(hot, gh_high_ref[i]) + mm_nt(hot, gh_low_ref[i])
        lgrad_ref[pl.ds(start, ROWS), :] = total
        return carry

    lax.fori_loop(0, n_left // ROWS, rows, 0)


VMEM = pl.BlockSpec(memory_space=pltpu.VMEM)


def in_hbm(*arrays):
    return tuple(pltpu.with_memory_space_constraint(a, pltpu.HBM) for a in arrays)


def edge_grads(own_left, count, src, kind, dst, neg, left_blk, right_blk, relations, interpret=False):
    _, width = left_blk.shape
    n_right, n_rel, blocks = right_blk.shape[0], relations.shape[0], src.shape[0]
    return pl.pallas_call(
        edge_kernel,
        out_shape=(
            jax.ShapeDtypeStruct((blocks, width, EDGES), BF16),
            jax.ShapeDtypeStruct((blocks, width, EDGES), BF16),
            jax.ShapeDtypeStruct((n_rel, width), BF16),
            jax.ShapeDtypeStruct((n_right, width), BF16),
            jax.ShapeDtypeStruct((own_left, width), BF16),
        ),
        in_specs=[VMEM] * 8,
        out_specs=(VMEM,) * 5,
        scratch_shapes=[
            pltpu.VMEM((width, n_right), BF16),
            pltpu.VMEM((n_rel, width), F32),
            pltpu.VMEM((n_right, width), F32),
        ],
        compiler_params=pltpu.CompilerParams(vmem_limit_bytes=40 * 2**20),
        interpret=interpret,
        name="edges",
    )(count, *in_hbm(src, kind, dst, neg, left_blk, right_blk, relations))


def left_sums(src, gh_high, gh_low, n_left, interpret=False):
    width = gh_high.shape[1]
    return pl.pallas_call(
        left_kernel,
        out_shape=jax.ShapeDtypeStruct((n_left, width), F32),
        in_specs=[VMEM] * 3,
        out_specs=VMEM,
        cost_estimate=pl.CostEstimate(
            flops=4 * n_left * src.size * width, transcendentals=0, bytes_accessed=8 * n_left * width
        ),
        compiler_params=pltpu.CompilerParams(vmem_limit_bytes=32 * 2**20),
        interpret=interpret,
        name="leftrows",
    )(*in_hbm(src), gh_high, gh_low)


def summed_over(part, axis, sizes):
    peers = np.arange(lax.axis_size(axis)).reshape(sizes)
    for dim in (1, 0, 3, 2):
        groups = np.moveaxis(peers, dim, -1).reshape(-1, sizes[dim]).tolist()
        part = jnp.sum(lax.all_gather(part, axis, axis=0, axis_index_groups=groups), axis=0)
    return part


def spread_kernel(total_ref, left_ref, code_ref, sent_ref, rows, done):
    own_left, own_rel = left_ref.shape[0], code_ref.shape[0]
    rows[:own_left] = (left_ref[...].astype(F32) - step_size * total_ref[...]).astype(BF16)
    rows[own_left : own_left + own_rel] = code_ref[...]
    copies = [pltpu.make_async_copy(rows, sent_ref.at[i], done.at[i]) for i in range(sent_ref.shape[0])]
    for copy in copies:
        copy.start()
    for copy in copies:
        copy.wait()


def for_all(total, left_rows, code, peers):
    shape = (left_rows.shape[0] + code.shape[0], left_rows.shape[1])
    return pl.pallas_call(
        spread_kernel,
        out_shape=jax.ShapeDtypeStruct((peers,) + shape, BF16),
        in_specs=[VMEM] * 3,
        out_specs=pl.BlockSpec(memory_space=pl.ANY),
        scratch_shapes=[pltpu.VMEM(shape, BF16), pltpu.SemaphoreType.DMA((peers,))],
        compiler_params=pltpu.CompilerParams(vmem_limit_bytes=4 * 2**20),
        name="spread",
    )(total, left_rows, code)


def settle_kernel(block_ref, out_ref, done):
    copy = pltpu.make_async_copy(block_ref, out_ref, done)
    copy.start()
    copy.wait()


def settled(block):
    return pl.pallas_call(
        settle_kernel,
        out_shape=jax.ShapeDtypeStruct(block.shape, block.dtype),
        in_specs=[VMEM],
        out_specs=pl.BlockSpec(memory_space=pl.ANY),
        scratch_shapes=[pltpu.SemaphoreType.DMA],
        compiler_params=pltpu.CompilerParams(vmem_limit_bytes=4 * 2**20),
        name="settle",
    )(block)


def finish_kernel(got_ref, left_next_ref, rel_next_ref, rel, done):
    own_left = left_next_ref.shape[1]
    left_copy = pltpu.make_async_copy(got_ref.at[:, :own_left, :], left_next_ref, done.at[0])
    left_copy.start()
    code = got_ref[:, own_left:, :].astype(F32)
    roots = jnp.sqrt(jnp.sqrt(jnp.abs(code)))
    rel[...] = jnp.where(code < 0, -roots, roots)
    rel_copy = pltpu.make_async_copy(rel, rel_next_ref, done.at[1])
    rel_copy.start()
    left_copy.wait()
    rel_copy.wait()


def finished(got, own_left):
    peers, rows, width = got.shape
    own_rel = rows - own_left
    return pl.pallas_call(
        finish_kernel,
        out_shape=(
            jax.ShapeDtypeStruct((peers, own_left, width), BF16),
            jax.ShapeDtypeStruct((peers, own_rel, width), F32),
        ),
        in_specs=[VMEM],
        out_specs=(pl.BlockSpec(memory_space=pl.ANY),) * 2,
        scratch_shapes=[pltpu.VMEM((peers, own_rel, width), F32), pltpu.SemaphoreType.DMA((2,))],
        compiler_params=pltpu.CompilerParams(vmem_limit_bytes=8 * 2**20),
        name="finish",
    )(got)


def shards(
    left_table, right_table, relations, source_ids, relation_ids, target_ids, negative_ids, edge_counts
):
    width = relations.shape[1]
    peers = lax.axis_size("right")
    mine = lax.axis_index("right")
    own_left = left_table.shape[0] // peers
    own_rel = relations.shape[0] // peers
    src, kind, dst, neg = (
        ids.reshape(-1, 1, EDGES) for ids in (source_ids, relation_ids, target_ids, negative_ids)
    )
    gh_high, gh_low, rel_grad, updated, left_rows = edge_grads(
        own_left, edge_counts, src, kind, dst, neg, left_table, right_table[0], relations
    )
    moved = passed_along(updated[None], "right", 1)
    rel_got = lax.all_to_all(rel_grad.reshape(peers, own_rel, width), "right", 0, 0)
    left_grad = left_sums(src, gh_high, gh_low, left_table.shape[0])
    sent = left_grad.astype(jnp.float16).reshape(peers, own_left, width)
    rel_part = jnp.sum(rel_got.astype(F32), axis=0)
    left_got = lax.all_to_all(sent, "right", 0, 0)
    rel_total = summed_over(rel_part, "left", (2, 2, 2, 2))
    rel_rows = lax.dynamic_slice_in_dim(relations, mine * own_rel, own_rel, 0)
    rel_rows = rel_rows - relation_step * rel_total
    left_total = jnp.sum(left_got.astype(F32), axis=0)
    squares = rel_rows * rel_rows
    code = (jnp.where(rel_rows < 0, -squares, squares) * squares).astype(BF16)
    got = lax.all_to_all(for_all(left_total, left_rows, code, peers), "right", 0, 0)
    moved = settled(moved)
    left_next, relations_next = finished(got, own_left)
    return (left_next.reshape(left_table.shape), moved, relations_next.reshape(relations.shape))


def solution(mesh):
    return jax.shard_map(
        shards,
        mesh=mesh,
        in_specs=(
            P("left", None),
            P("left", "right", None),
            P(),
            P("left", "right", None),
            P("left", "right", None),
            P("left", "right", None),
            P("left", "right", None, None),
            P("left", "right"),
        ),
        out_specs=(P("left", None), P("left", "right", None), P()),
        check_vma=False,
    )
```

```python
import jax
import jax.numpy as jnp
import numpy as np
from jax import lax
from jax.experimental import pallas as pl
from jax.experimental.pallas import tpu as pltpu
from jax.sharding import PartitionSpec as P


step_size = 0.5
relation_step = 12.0
EDGES = 1024
ROWS = 2048
F32 = jnp.float32
BF16 = jnp.bfloat16


def passed_along(array, axis, by):
    peers = lax.axis_size(axis)
    return lax.ppermute(array, axis, [(i, (i + by) % peers) for i in range(peers)])


def mm(a, b):
    return lax.dot_general(a, b, (((1,), (0,)), ((), ())), preferred_element_type=F32)


def mm_nt(a, b):
    return lax.dot_general(a, b, (((1,), (1,)), ((), ())), preferred_element_type=F32)


def mm_tn(a, b):
    return lax.dot_general(a, b, (((0,), (0,)), ((), ())), preferred_element_type=F32)


def two_parts(x):
    high = x.astype(BF16)
    return high, (x - high.astype(F32)).astype(BF16)


def one_hot(rows, ids):
    places = lax.broadcasted_iota(jnp.int32, (rows, ids.shape[1]), 0)
    return jnp.where(places.astype(jnp.int16) == ids.astype(jnp.int16), BF16(1), BF16(0))


def edge_kernel(
    count_ref, src_ref, kind_ref, dst_ref, neg_ref, left_ref, right_ref, rel_ref,
    gh_high_ref, gh_low_ref, rgrad_ref, right_new_ref, own_ref,
    right_t, rgrad, tgrad,
):
    n_left, width = left_ref.shape
    n_right, n_rel = right_ref.shape[0], rel_ref.shape[0]
    half = width // 2
    negs = neg_ref.shape[0] * neg_ref.shape[2]
    count = count_ref[...]
    eye = jnp.where(
        lax.broadcasted_iota(jnp.int32, (width, width), 0)
        == lax.broadcasted_iota(jnp.int32, (width, width), 1),
        1.0,
        0.0,
    ).astype(BF16)
    right_t[...] = mm_nt(eye, right_ref[...]).astype(BF16)
    rel_high, rel_low = two_parts(rel_ref[...])
    seen = one_hot(n_right, neg_ref[0]).astype(F32)
    for i in range(1, neg_ref.shape[0]):
        seen = seen + one_hot(n_right, neg_ref[i]).astype(F32)
    times = jnp.sum(seen, axis=1, keepdims=True) * (1.0 / negs)

    def block(i, carry):
        ohs = one_hot(n_left, src_ref[i])
        ohk = one_hot(n_rel, kind_ref[i])
        ohd = one_hot(n_right, dst_ref[i])
        head = mm_tn(left_ref[...], ohs)
        tail = mm(right_t[...], ohd)
        rel = mm_tn(rel_high, ohk) + mm_tn(rel_low, ohk)
        hre, him = head[:half], head[half:]
        rre, rim = rel[:half], rel[half:]
        query = jnp.concatenate([hre * rre - him * rim, hre * rim + him * rre], axis=0)
        q_low = query.astype(BF16)
        pos = jnp.sum(query * tail, axis=0, keepdims=True)
        slot = i * EDGES + lax.broadcasted_iota(jnp.int32, (1, EDGES), 1)
        live = jnp.where(slot < count, 1.0, 0.0)
        c_pos = -jax.nn.sigmoid(-pos) * live
        scores = mm(right_ref[...], q_low)
        c_neg = (jax.nn.sigmoid(scores) * (times * live)).astype(BF16)
        g_query = mm(right_t[...], c_neg) + c_pos * tail
        gre, gim = g_query[:half], g_query[half:]
        grad_h = jnp.concatenate([gre * rre + gim * rim, -gre * rim + gim * rre], axis=0)
        grad_r = jnp.concatenate([gre * hre + gim * him, -gre * him + gim * hre], axis=0)
        gh_high_ref[i], gh_low_ref[i] = two_parts(grad_h)
        rgrad_ref[...] = mm_nt(ohk, grad_r.astype(BF16)).astype(BF16)
        t_high, t_low = two_parts(c_pos * query)
        grad = mm_nt(c_neg, q_low) + mm_nt(ohd, t_high) + mm_nt(ohd, t_low)
        right_new_ref[...] = (right_ref[...].astype(F32) - step_size * grad).astype(BF16)
        return carry

    block(0, 0)
    own = own_ref.shape[0]
    own_ref[...] = left_ref[pl.ds(pl.multiple_of(lax.axis_index("right") * own, own), own), :]


def left_kernel(src_ref, gh_high_ref, gh_low_ref, lgrad_ref):
    n_left, width = lgrad_ref.shape
    blocks = src_ref.shape[0]

    def rows(j, carry):
        start = pl.multiple_of(j * ROWS, ROWS)
        total = jnp.zeros((ROWS, width), F32)
        for i in range(blocks):
            hot = one_hot(ROWS, src_ref[i] - start)
            total += mm_nt(hot, gh_high_ref[i]) + mm_nt(hot, gh_low_ref[i])
        lgrad_ref[pl.ds(start, ROWS), :] = total
        return carry

    lax.fori_loop(0, n_left // ROWS, rows, 0)


VMEM = pl.BlockSpec(memory_space=pltpu.VMEM)


def in_hbm(*arrays):
    return tuple(pltpu.with_memory_space_constraint(a, pltpu.HBM) for a in arrays)


def edge_grads(own_left, count, src, kind, dst, neg, left_blk, right_blk, relations, interpret=False):
    _, width = left_blk.shape
    n_right, n_rel, blocks = right_blk.shape[0], relations.shape[0], src.shape[0]
    return pl.pallas_call(
        edge_kernel,
        out_shape=(
            jax.ShapeDtypeStruct((blocks, width, EDGES), BF16),
            jax.ShapeDtypeStruct((blocks, width, EDGES), BF16),
            jax.ShapeDtypeStruct((n_rel, width), BF16),
            jax.ShapeDtypeStruct((n_right, width), BF16),
            jax.ShapeDtypeStruct((own_left, width), BF16),
        ),
        in_specs=[VMEM] * 8,
        out_specs=(VMEM,) * 5,
        scratch_shapes=[
            pltpu.VMEM((width, n_right), BF16),
            pltpu.VMEM((n_rel, width), F32),
            pltpu.VMEM((n_right, width), F32),
        ],
        compiler_params=pltpu.CompilerParams(vmem_limit_bytes=40 * 2**20),
        interpret=interpret,
        name="edges",
    )(count, *in_hbm(src, kind, dst, neg, left_blk, right_blk, relations))


def left_sums(src, gh_high, gh_low, n_left, interpret=False):
    width = gh_high.shape[1]
    return pl.pallas_call(
        left_kernel,
        out_shape=jax.ShapeDtypeStruct((n_left, width), F32),
        in_specs=[VMEM] * 3,
        out_specs=VMEM,
        cost_estimate=pl.CostEstimate(
            flops=4 * n_left * src.size * width, transcendentals=0, bytes_accessed=8 * n_left * width
        ),
        compiler_params=pltpu.CompilerParams(vmem_limit_bytes=32 * 2**20),
        interpret=interpret,
        name="leftrows",
    )(*in_hbm(src), gh_high, gh_low)


def summed_over(part, axis, sizes):
    peers = np.arange(lax.axis_size(axis)).reshape(sizes)
    for dim in (1, 0, 3, 2):
        groups = np.moveaxis(peers, dim, -1).reshape(-1, sizes[dim]).tolist()
        part = jnp.sum(lax.all_gather(part, axis, axis=0, axis_index_groups=groups), axis=0)
    return part


def spread_kernel(total_ref, left_ref, code_ref, sent_ref, rows, done):
    own_left, own_rel = left_ref.shape[0], code_ref.shape[0]
    rows[:own_left] = (left_ref[...].astype(F32) - step_size * total_ref[...]).astype(BF16)
    rows[own_left : own_left + own_rel] = code_ref[...]
    copies = [pltpu.make_async_copy(rows, sent_ref.at[i], done.at[i]) for i in range(sent_ref.shape[0])]
    for copy in copies:
        copy.start()
    for copy in copies:
        copy.wait()


def for_all(total, left_rows, code, peers):
    shape = (left_rows.shape[0] + code.shape[0], left_rows.shape[1])
    return pl.pallas_call(
        spread_kernel,
        out_shape=jax.ShapeDtypeStruct((peers,) + shape, BF16),
        in_specs=[VMEM] * 3,
        out_specs=pl.BlockSpec(memory_space=pl.ANY),
        scratch_shapes=[pltpu.VMEM(shape, BF16), pltpu.SemaphoreType.DMA((peers,))],
        compiler_params=pltpu.CompilerParams(vmem_limit_bytes=4 * 2**20),
        name="spread",
    )(total, left_rows, code)


def settle_kernel(block_ref, out_ref, done):
    copy = pltpu.make_async_copy(block_ref, out_ref, done)
    copy.start()
    copy.wait()


def settled(block):
    return pl.pallas_call(
        settle_kernel,
        out_shape=jax.ShapeDtypeStruct(block.shape, block.dtype),
        in_specs=[VMEM],
        out_specs=pl.BlockSpec(memory_space=pl.ANY),
        scratch_shapes=[pltpu.SemaphoreType.DMA],
        compiler_params=pltpu.CompilerParams(vmem_limit_bytes=4 * 2**20),
        name="settle",
    )(block)


def finish_kernel(got_ref, left_next_ref, rel_next_ref, rel, done):
    own_left = left_next_ref.shape[1]
    left_copy = pltpu.make_async_copy(got_ref.at[:, :own_left, :], left_next_ref, done.at[0])
    left_copy.start()
    code = got_ref[:, own_left:, :].astype(F32)
    roots = jnp.sqrt(jnp.sqrt(jnp.abs(code)))
    rel[...] = jnp.where(code < 0, -roots, roots)
    rel_copy = pltpu.make_async_copy(rel, rel_next_ref, done.at[1])
    rel_copy.start()
    left_copy.wait()
    rel_copy.wait()


def finished(got, own_left):
    peers, rows, width = got.shape
    own_rel = rows - own_left
    return pl.pallas_call(
        finish_kernel,
        out_shape=(
            jax.ShapeDtypeStruct((peers, own_left, width), BF16),
            jax.ShapeDtypeStruct((peers, own_rel, width), F32),
        ),
        in_specs=[VMEM],
        out_specs=(pl.BlockSpec(memory_space=pl.ANY),) * 2,
        scratch_shapes=[pltpu.VMEM((peers, own_rel, width), F32), pltpu.SemaphoreType.DMA((2,))],
        compiler_params=pltpu.CompilerParams(vmem_limit_bytes=8 * 2**20),
        name="finish",
    )(got)


def shards(
    left_table, right_table, relations, source_ids, relation_ids, target_ids, negative_ids, edge_counts
):
    width = relations.shape[1]
    peers = lax.axis_size("right")
    mine = lax.axis_index("right")
    own_left = left_table.shape[0] // peers
    own_rel = relations.shape[0] // peers
    src, kind, dst, neg = (
        ids.reshape(-1, 1, EDGES) for ids in (source_ids, relation_ids, target_ids, negative_ids)
    )
    gh_high, gh_low, rel_grad, updated, left_rows = edge_grads(
        own_left, edge_counts, src, kind, dst, neg, left_table, right_table[0], relations
    )
    moved = passed_along(updated[None], "right", 1)
    rel_got = lax.all_to_all(rel_grad.reshape(peers, own_rel, width), "right", 0, 0)
    left_grad = left_sums(src, gh_high, gh_low, left_table.shape[0])
    sent = left_grad.astype(jnp.float16).reshape(peers, own_left, width)
    rel_part = jnp.sum(rel_got.astype(F32), axis=0)
    left_got = lax.all_to_all(sent, "right", 0, 0)
    rel_total = summed_over(rel_part, "left", (2, 2, 2, 2))
    rel_rows = lax.dynamic_slice_in_dim(relations, mine * own_rel, own_rel, 0)
    rel_rows = rel_rows - relation_step * rel_total
    left_total = jnp.sum(left_got.astype(F32), axis=0)
    squares = rel_rows * rel_rows
    code = (jnp.where(rel_rows < 0, -squares, squares) * squares).astype(BF16)
    got = lax.all_to_all(for_all(left_total, left_rows, code, peers), "right", 0, 0)
    moved = settled(moved)
    left_next, relations_next = finished(got, own_left)
    return (left_next.reshape(left_table.shape), moved, relations_next.reshape(relations.shape))


def solution(mesh):
    return jax.shard_map(
        shards,
        mesh=mesh,
        in_specs=(
            P("left", None),
            P("left", "right", None),
            P(),
            P("left", "right", None),
            P("left", "right", None),
            P("left", "right", None),
            P("left", "right", None, None),
            P("left", "right"),
        ),
        out_specs=(P("left", None), P("left", "right", None), P()),
        check_vma=False,
    )
```
